256 devices in a mesh: layer: 16 (over z_lo, y), lat: 16 (over z_hi, x, core).
Axes of the slice: x: 4, y: 4, z: 8 (z_hi: 2, z_lo: 4; z = z_hi * 4 + z_lo), core: 2. Of those that a mesh axis runs over, the one named last changes fastest.
Arguments:
- inputs: bfloat16 [128, 4, 2048], P(None, None, 'layer'), may hold values from -6 to 6
- encoder: bfloat16 [4, 2048, 16384], P(None, 'layer', 'lat'), may hold values from -0.125 to 0.125
- enc_bias: float32 [4, 16384], P(None, 'lat'), may hold values from -3 to 3
- decoder: bfloat16 [16, 5, 16384, 256], P('layer', None, 'lat'), may hold values from -0.375 to 0.375
- dec_bias: float32 [16, 2, 256], P('layer'), may hold values from -3 to 3
- targets: bfloat16 [16, 128, 2, 256], P('layer'), may hold values from -6 to 6
- top_index: int32 [128, 4, 64], replicated, may hold values from 0 to 16383, as said below
Outputs:
- decoder_grad: float32 [16, 5, 16384, 256], P('layer', None, 'lat')
- encoder_grad: float32 [4, 2048, 16384], P(None, 'layer', 'lat')
- bias_grad: float32 [4, 16384], P(None, 'lat')
The draws below stay inside these ranges and needn't reach their ends.
Inputs may be any that keep to these rules, and one draw needn't show every extreme that they name: `top_index`: the 64 entries of one token and layer are distinct; at most 8 of them have the same value of n // 1024, and every value of n // 1024 is taken by exactly 8 entries of some token and layer.
All inputs are finite; a program needn't handle non-finite values.
Results may differ from the reference program's by a relative error of at most 0.0045.
Values may be sent and summed in bfloat16 or wider, within the bound.
A program may use at most 64 MiB of HBM per device.

```python
import jax
import jax.numpy as jnp
from jax import lax

D = 2048
LAT_DEV = 1024
LATENTS = 16384
TOKENS = 128
TOPK = 64
SLAB_MOST = 8
FEAT_SPLIT = 8
FEAT_BLK = 256
LAYERS = 4
N_LAYER = 16


def draw_top_index(key, part):
    group_count = LATENTS // LAT_DEV
    cell_count = group_count * SLAB_MOST
    row_count = TOKENS * LAYERS
    key_list = jax.random.split(jax.random.fold_in(key, 7101), 5)
    offset = jax.random.randint(key_list[0], (), 0, group_count)
    full_group = (jnp.arange(row_count, dtype=jnp.int32) + offset) % group_count
    cell_ids = jnp.arange(cell_count, dtype=jnp.int32)
    cell_group = cell_ids // SLAB_MOST
    scores = jax.random.randint(key_list[1], (row_count, cell_count), 0, 2 ** 20)
    scores = scores + jnp.where(cell_group[None, :] == full_group[:, None], 2 ** 21, 0)
    scores = scores * cell_count + cell_ids[None, :]
    unused, chosen = lax.top_k(scores, TOPK)
    order_key = jax.random.randint(key_list[2], (row_count, TOPK), 0, 2 ** 20) * TOPK + jnp.arange(TOPK, dtype=jnp.int32)[None, :]
    ordering = jnp.argsort(order_key, axis=1)
    chosen = jnp.take_along_axis(chosen, ordering, axis=1)
    chosen_group = chosen // SLAB_MOST
    chosen_rank = chosen % SLAB_MOST
    base_offset = jax.random.randint(key_list[3], (row_count, group_count), 0, LAT_DEV)
    stride = 2 * jax.random.randint(key_list[4], (row_count, group_count), 0, LAT_DEV // 2) + 1
    group_base = jnp.take_along_axis(base_offset, chosen_group, axis=1)
    group_stride = jnp.take_along_axis(stride, chosen_group, axis=1)
    latent = chosen_group * LAT_DEV + (group_base + chosen_rank * group_stride) % LAT_DEV
    return latent.reshape(TOKENS, LAYERS, TOPK).astype(jnp.int32)


def levels(stream_key, extent, pieces, least, high):
    level = 1.0
    for position, parts in pieces:
        steps = jax.random.uniform(jax.random.fold_in(jax.random.fold_in(stream_key, 6), position), (parts,), jnp.float32, least / len(pieces), high / len(pieces))
        level = level * jnp.repeat(jnp.exp(steps), extent[position] // parts).reshape((-1,) + (1,) * (len(extent) - 1 - position))
    return level


def gaussian(key, extent, scale, most, pieces=(), held_as=jnp.bfloat16):
    array = jax.random.normal(key, extent, jnp.float32) * scale
    if len(pieces) > 0:
        array = levels(key, extent, pieces, -0.22, 0.18) * array
    return jnp.clip(array, min=-most, max=most).astype(held_as)


def setup_inputs(seed: int = 0) -> dict:
    streams_of = jax.random.split(jax.random.key(seed), 8)
    return {
        "inputs": gaussian(streams_of[0], (TOKENS, LAYERS, D), 1.0, 6.0, ((2, 16),)),
        "encoder": gaussian(streams_of[1], (LAYERS, D, LATENTS), D ** -0.5, 0.125, ((1, 16), (2, 16))),
        "enc_bias": gaussian(streams_of[2], (LAYERS, LATENTS), 0.5, 3.0, ((1, 16),), jnp.float32),
        "decoder": gaussian(streams_of[3], (N_LAYER, LAYERS + 1, LATENTS, FEAT_BLK), (TOPK * LAYERS) ** -0.5, 0.375, ((0, 16), (2, 16))),
        "dec_bias": gaussian(streams_of[4], (N_LAYER, 2, FEAT_BLK), 0.5, 3.0, ((0, 16),), jnp.float32),
        "targets": gaussian(streams_of[5], (N_LAYER, TOKENS, 2, FEAT_BLK), 1.0, 6.0, ((0, 16),)),
        "top_index": draw_top_index(jax.random.fold_in(streams_of[7], 71), 0),
    }


def reference(inputs, encoder, enc_bias, decoder, dec_bias, targets, top_index):
    pre_values = []
    for layer_id in range(LAYERS):
        picked = top_index[:, layer_id, :]
        columns = jnp.take(encoder[layer_id].T, picked, axis=0)
        values = jnp.einsum("td,tkd->tk", inputs[:, layer_id, :].astype(jnp.float32), columns.astype(jnp.float32))
        values = values + jnp.take(enc_bias[layer_id], picked, axis=0)
        pre_values.append(lax.optimization_barrier(values.astype(jnp.bfloat16)))
    grad_values = [jnp.zeros((TOKENS, TOPK), jnp.float32) for layer_id in range(LAYERS)]
    decoder_rows = []
    for row_index in range(N_LAYER):
        pair_index = row_index // FEAT_SPLIT
        block_plan = []
        for block_index in range(LAYERS + 1):
            if block_index <= pair_index:
                block_plan.append((block_index, block_index, 0))
            else:
                block_plan.append((block_index, block_index - pair_index - 1, 1))
        gathered = {}
        slot_sums = [dec_bias[row_index, 0][None, :] + jnp.zeros((TOKENS, FEAT_BLK), jnp.float32),
                     dec_bias[row_index, 1][None, :] + jnp.zeros((TOKENS, FEAT_BLK), jnp.float32)]
        for block_index, source, slot_index in block_plan:
            row_weights = jnp.take(decoder[row_index, block_index], top_index[:, source, :], axis=0).astype(jnp.float32)
            gathered[block_index] = row_weights
            slot_sums[slot_index] = slot_sums[slot_index] + jnp.einsum("tk,tkf->tf", pre_values[source].astype(jnp.float32), row_weights)
        residues = []
        for slot_index in range(2):
            residue = slot_sums[slot_index] - targets[row_index, :, slot_index, :].astype(jnp.float32)
            residues.append(lax.optimization_barrier(residue.astype(jnp.bfloat16)))
        block_grads = []
        for block_index, source, slot_index in block_plan:
            residue = residues[slot_index].astype(jnp.float32)
            updates = pre_values[source].astype(jnp.float32)[:, :, None] * residue[:, None, :]
            block_grad = jnp.zeros((LATENTS, FEAT_BLK), jnp.float32).at[top_index[:, source, :]].add(updates)
            block_grads.append(block_grad)
            grad_values[source] = grad_values[source] + jnp.einsum("tf,tkf->tk", residue, gathered[block_index])
        decoder_rows.append(jnp.stack(block_grads, axis=0))
    decoder_grad = jnp.stack(decoder_rows, axis=0)
    encoder_layers = []
    bias_layers = []
    for layer_id in range(LAYERS):
        picked = top_index[:, layer_id, :]
        pre_grad = lax.optimization_barrier(grad_values[layer_id].astype(jnp.bfloat16)).astype(jnp.float32)
        updates = pre_grad[:, :, None] * inputs[:, layer_id, :].astype(jnp.float32)[:, None, :]
        transposed = jnp.zeros((LATENTS, D), jnp.float32).at[picked].add(updates)
        encoder_layers.append(transposed.T)
        bias_layers.append(jnp.zeros((LATENTS,), jnp.float32).at[picked].add(pre_grad))
    return decoder_grad, jnp.stack(encoder_layers, axis=0), jnp.stack(bias_layers, axis=0)
```

```python
import jax
import jax.numpy as jnp
from jax import lax
from jax.experimental import pallas as pl
from jax.experimental.pallas import tpu as pltpu
from jax.sharding import PartitionSpec as P

MESH = pl.DeviceIdType.MESH
F32 = jnp.float32
BF16 = jnp.bfloat16
I32 = jnp.int32

TOKENS, LAYERS, TOPK, WIDTH, DIN, FEAT, BLOCKS, SLOTS = 128, 4, 64, 1024, 128, 256, 5, 8
WIRE = F32


def pick(values, lanes):
    return jnp.take_along_axis(values, lanes, axis=1, mode="promise_in_bounds")


def main_kernel(x_hbm, enc_hbm, bias_hbm, dec_hbm, dbias_hbm, tgt_hbm, idx_hbm,
                act_ref, res_ref, pg_ref, xt_ref,
                x_v, enc_v, bias_v, dec_v, dbias_v, tgt_v, idx_v, load_sem,
                xf, dense, inv, code_v, low_v, high_v, rec, goal,
                ybuf1, zbuf1, ybuf2, zbuf2, rs_src, rs_buf, hbuf, abuf, val_v,
                y1_s, y1_r, z1_s, z1_r, y2_s, y2_r, z2_s, z2_r,
                rs_s, rs_r, h_s, h_r, ag_s, ag_r):
    r = lax.axis_index("layer")
    j = lax.axis_index("lat")
    y = lax.rem(r, 4)
    zl = lax.div(r, 4)
    q = lax.rem(j, 8)
    zh = lax.div(j, 8)
    g = lax.div(r, 8)

    loads = [
        pltpu.make_async_copy(idx_hbm, idx_v, load_sem.at[0]),
        pltpu.make_async_copy(x_hbm, x_v, load_sem.at[1]),
        pltpu.make_async_copy(enc_hbm, enc_v, load_sem.at[2]),
        pltpu.make_async_copy(bias_hbm, bias_v, load_sem.at[3]),
        pltpu.make_async_copy(dec_hbm, dec_v, load_sem.at[4]),
        pltpu.make_async_copy(dbias_hbm, dbias_v, load_sem.at[5]),
        pltpu.make_async_copy(tgt_hbm.at[pl.ds(q * 16, 16)], tgt_v, load_sem.at[6]),
    ]
    for copy in loads:
        copy.start()

    def ypeer(i):
        return {"layer": zl * 4 + lax.rem(y + i, 4)}

    def zpeer(i):
        return {"layer": lax.rem(zl + i, 4) * 4 + y}

    def qpeer(i):
        return {"lat": zh * 8 + lax.rem(q + i, 8)}

    hpeer = {"lat": (1 - zh) * 8 + q}

    barrier = pltpu.get_barrier_semaphore()
    for i in range(1, 4):
        pl.semaphore_signal(barrier, inc=1, device_id=ypeer(i), device_id_type=MESH)
        pl.semaphore_signal(barrier, inc=1, device_id=zpeer(i), device_id_type=MESH)
    for i in range(1, 8):
        pl.semaphore_signal(barrier, inc=1, device_id=qpeer(i), device_id_type=MESH)
    pl.semaphore_signal(barrier, inc=1, device_id=hpeer, device_id_type=MESH)

    lane = lax.broadcasted_iota(I32, (32, 128), 1)
    quarter = lax.shift_right_logical(lane, 5)

    loads[0].wait()
    tri = (lax.broadcasted_iota(I32, (TOPK, TOPK), 1)
           < lax.broadcasted_iota(I32, (TOPK, TOPK), 0)).astype(F32).astype(BF16)
    sub8 = lax.broadcasted_iota(I32, (SLOTS, 128), 0)
    packs = []
    for l in range(LAYERS):
        local = idx_v[l] - j * WIDTH
        inside = (local >= 0) & (local < WIDTH)
        rank = jnp.dot(tri, inside.astype(F32).astype(BF16), preferred_element_type=F32)
        rank = jnp.where(inside, rank, -1.0)
        value = (local + (l * WIDTH + 1)).astype(F32)
        slot_rows = jnp.zeros((SLOTS, 128), F32)
        for s in range(SLOTS):
            row = jnp.sum(jnp.where(rank == float(s), value, 0.0), axis=0, keepdims=True)
            slot_rows = jnp.where(sub8 == s, row, slot_rows)
        packs.append(slot_rows)
    packed = jnp.concatenate(packs * 4, axis=0)
    code = jnp.transpose(packed).astype(I32) - 1
    code_v[...] = code
    low_v[...] = code & 127
    high_v[...] = lax.shift_right_arithmetic(code, 7)

    loads[1].wait()
    loads[2].wait()
    loads[3].wait()
    xf[...] = x_v[...].astype(F32)
    own = jnp.where(r == 0, 1.0, 0.0)
    for l in range(LAYERS):
        x_l = xf[pl.ds(l, TOKENS, stride=4), :]
        dense[l] = (jnp.dot(x_l.astype(BF16), enc_v[l], preferred_element_type=F32)
                    + bias_v[pl.ds(l, 1), :] * own)

    def gather():
        def step(tq, out):
            rows = pl.ds(pl.multiple_of(tq * 32, 32), 32)
            low = low_v[rows, :]
            high = high_v[rows, :]
            got = jnp.zeros((32, 128), F32)
            for b in range(32):
                block = dense[b // 8, rows, pl.ds((b % 8) * 128, 128)]
                got = jnp.where(high == b, pick(block, low), got)
            return jnp.where(quarter == tq, got, out)

        return lax.fori_loop(0, 4, step, jnp.zeros((32, 128), F32))

    def scatter(out_ref):
        def step(tq, carry):
            rows = pl.ds(pl.multiple_of(tq * 32, 32), 32)
            values = val_v[...]
            for b in range(32):
                cols = pl.ds((b % 8) * 128, 128)
                where = inv[b // 8, rows, cols]
                got = jnp.where(where >= 0, pick(values, where & 127), 0.0)
                out_ref[b // 8, rows, cols] = got.astype(BF16)
            return carry

        lax.fori_loop(0, 4, step, 0)

    def send(src, dst, s_sem, r_sem, peer):
        copy = pltpu.make_async_remote_copy(
            src_ref=src, dst_ref=dst, send_sem=s_sem, recv_sem=r_sem,
            device_id=peer, device_id_type=MESH)
        copy.start()
        return copy

    def exchange(buf, me, n, peer, s_sem, r_sem, between=None):
        sends = [send(buf.at[me], buf.at[me], s_sem.at[i], r_sem.at[me], peer(i))
                 for i in range(n - 1, 0, -1)]
        if between is not None:
            between()
        for i in range(1, n):
            other = lax.rem(me + i, n)
            pltpu.make_async_remote_copy(
                src_ref=buf.at[other], dst_ref=buf.at[other], send_sem=s_sem.at[i],
                recv_sem=r_sem.at[other], device_id=peer(i), device_id_type=MESH).wait_recv()
        for copy in sends:
            copy.wait_send()

    def total(buf, n):
        acc = buf[0].astype(F32)
        for i in range(1, n):
            acc = acc + buf[i].astype(F32)
        return acc

    def build_inverse():
        def step(c, carry):
            rows = pl.ds(pl.multiple_of(c * 16, 16), 16)
            base = lax.div(c, 2) * 32
            lane16 = lax.broadcasted_iota(I32, (16, 128), 1)
            code_rows = code_v[rows, :]
            for l in range(LAYERS):
                found = [jnp.full((16, 128), -1, I32) for h in range(8)]
                for s in range(SLOTS):
                    col = l * SLOTS + s
                    at = jnp.broadcast_to(code_rows[:, col:col + 1], (16, 128)) - l * WIDTH
                    for h in range(8):
                        found[h] = jnp.where(at == lane16 + h * 128, base + col, found[h])
                for h in range(8):
                    inv[l, rows, pl.ds(h * 128, 128)] = found[h]
            return carry

        lax.fori_loop(0, 8, step, 0)
        loads[5].wait()
        loads[6].wait()
        goal_all = tgt_v[...].astype(F32)
        for c in range(2):
            goal[c] = goal_all[:, c, :]

    def transpose_inputs():
        for l in range(LAYERS):
            xt_ref[l] = jnp.transpose(xf[pl.ds(l, TOKENS, stride=4), :]).astype(BF16)

    ybuf1[y] = gather().astype(WIRE)
    pl.semaphore_wait(barrier, 14)
    exchange(ybuf1, y, 4, ypeer, y1_s, y1_r, between=build_inverse)
    zbuf1[zl] = total(ybuf1, 4).astype(WIRE)
    exchange(zbuf1, zl, 4, zpeer, z1_s, z1_r, between=transpose_inputs)
    val_v[...] = total(zbuf1, 4).astype(BF16).astype(F32)
    scatter(act_ref)

    loads[4].wait()
    first = jnp.where(g == 1, 0, 1)

    def source_of(k):
        return jnp.where(k <= g, k, k - g - 1)

    def slot_of(k):
        return jnp.where(k <= g, 0, 1)

    def rebuild(k):
        return jnp.dot(act_ref[source_of(k)], dec_v[k], preferred_element_type=F32)

    rec[0] = rebuild(0)
    rec[1] = rebuild(2) + rebuild(3) + rebuild(4)
    rec[first] = rec[first] + rebuild(1)
    for c in range(2):
        rs_src[:, c] = rec[c].reshape(8, 16, FEAT).astype(BF16)
    rs_buf[q] = rs_src[q]
    sends = []
    for i in (4, 3, 5, 2, 6, 1, 7):
        other = lax.rem(q + i, 8)
        sends.append(send(rs_src.at[other], rs_buf.at[q], rs_s.at[i], rs_r.at[q], qpeer(i)))
    dense[...] = jnp.zeros_like(dense)
    for i in range(1, 8):
        other = lax.rem(q + i, 8)
        pltpu.make_async_remote_copy(
            src_ref=rs_buf.at[other], dst_ref=rs_buf.at[other], send_sem=rs_s.at[i],
            recv_sem=rs_r.at[other], device_id=qpeer(i), device_id_type=MESH).wait_recv()
    for copy in sends:
        copy.wait_send()
    hbuf[zh] = total(rs_buf, 8).astype(hbuf.dtype)
    copy = send(hbuf.at[zh], hbuf.at[zh], h_s, h_r.at[zh], hpeer)
    pltpu.make_async_remote_copy(
        src_ref=hbuf.at[1 - zh], dst_ref=hbuf.at[1 - zh], send_sem=h_s,
        recv_sem=h_r.at[1 - zh], device_id=hpeer, device_id_type=MESH).wait_recv()
    copy.wait_send()
    rebuilt = total(hbuf, 2)
    for c in range(2):
        abuf[q, c] = (rebuilt[c] + dbias_v[pl.ds(c, 1), :] - goal[c]).astype(BF16)
    exchange(abuf, q, 8, qpeer, ag_s, ag_r)

    for k in range(BLOCKS):
        residue = abuf[:, slot_of(k)].reshape(TOKENS, FEAT)
        dense[source_of(k)] = dense[source_of(k)] + lax.dot_general(
            residue, dec_v[k], (((1,), (1,)), ((), ())), preferred_element_type=F32)
    ybuf2[y] = gather().astype(WIRE)
    def keep_residue():
        res_ref[...] = abuf[...]

    exchange(ybuf2, y, 4, ypeer, y2_s, y2_r, between=keep_residue)
    zbuf2[zl] = total(ybuf2, 4).astype(WIRE)
    exchange(zbuf2, zl, 4, zpeer, z2_s, z2_r)
    val_v[...] = total(zbuf2, 4).astype(BF16).astype(F32)
    scatter(pg_ref)


def main_call(x, enc, bias, dec, dbias, tgt, idx):
    dma = pltpu.SemaphoreType.DMA
    vmem = pltpu.VMEM
    return pl.pallas_call(
        main_kernel,
        out_shape=(
            jax.ShapeDtypeStruct((LAYERS, TOKENS, WIDTH), BF16),
            jax.ShapeDtypeStruct((8, 2, 16, FEAT), BF16),
            jax.ShapeDtypeStruct((LAYERS, TOKENS, WIDTH), BF16),
            jax.ShapeDtypeStruct((LAYERS, DIN, TOKENS), BF16),
        ),
        in_specs=[pl.BlockSpec(memory_space=pl.ANY)] * 7,
        out_specs=(pl.BlockSpec(memory_space=pltpu.VMEM),) * 4,
        scratch_shapes=[
            vmem((TOKENS * LAYERS, DIN), BF16),
            vmem((LAYERS, DIN, WIDTH), BF16),
            vmem((LAYERS, WIDTH), F32),
            vmem((BLOCKS, WIDTH, FEAT), BF16),
            vmem((2, FEAT), F32),
            vmem((16, 2, FEAT), BF16),
            vmem((LAYERS, TOPK, TOKENS), I32),
            dma((7,)),
            vmem((TOKENS * LAYERS, DIN), F32),
            vmem((LAYERS, TOKENS, WIDTH), F32),
            vmem((LAYERS, TOKENS, WIDTH), I32),
            vmem((TOKENS, 128), I32),
            vmem((TOKENS, 128), I32),
            vmem((TOKENS, 128), I32),
            vmem((2, TOKENS, FEAT), F32),
            vmem((2, 16, FEAT), F32),
            vmem((4, 32, 128), WIRE),
            vmem((4, 32, 128), WIRE),
            vmem((4, 32, 128), WIRE),
            vmem((4, 32, 128), WIRE),
            vmem((8, 2, 16, FEAT), BF16),
            vmem((8, 2, 16, FEAT), BF16),
            vmem((2, 2, 16, FEAT), WIRE),
            vmem((8, 2, 16, FEAT), BF16),
            vmem((32, 128), F32),
            dma((4,)), dma((4,)), dma((4,)), dma((4,)),
            dma((4,)), dma((4,)), dma((4,)), dma((4,)),
            dma((8,)), dma((8,)), dma, dma((2,)), dma((8,)), dma((8,)),
        ],
        compiler_params=pltpu.CompilerParams(collective_id=0, has_side_effects=True),
        name="transcoder",
    )(x, enc, bias, dec, dbias, tgt, idx)


def grad_kernel(act_ref, res_ref, pg_ref, xt_ref, dg_ref, eg_ref, bg_ref):
    k = pl.program_id(0)
    g = lax.div(lax.axis_index("layer"), 8)
    source = jnp.where(k <= g, k, k - g - 1)
    slot = jnp.where(k <= g, 0, 1)
    residue = res_ref[:, slot].reshape(TOKENS, FEAT)
    dg_ref[0] = lax.dot_general(act_ref[source], residue, (((0,), (0,)), ((), ())),
                                preferred_element_type=F32)

    @pl.when(k < LAYERS)
    def _():
        grads = pg_ref[k]
        eg_ref[0] = jnp.dot(xt_ref[k], grads, preferred_element_type=F32)
        bg_ref[pl.ds(k, 1), :] = jnp.dot(jnp.ones((8, TOKENS), BF16), grads,
                                         preferred_element_type=F32)[0:1]


def grad_call(act, res, pg, xt):
    def whole(*shape):
        return pl.BlockSpec(shape, lambda k: (0,) * len(shape))

    return pl.pallas_call(
        grad_kernel,
        grid=(BLOCKS,),
        out_shape=(
            jax.ShapeDtypeStruct((BLOCKS, WIDTH, FEAT), F32),
            jax.ShapeDtypeStruct((LAYERS, DIN, WIDTH), F32),
            jax.ShapeDtypeStruct((LAYERS, WIDTH), F32),
        ),
        in_specs=[whole(LAYERS, TOKENS, WIDTH), whole(8, 2, 16, FEAT),
                  whole(LAYERS, TOKENS, WIDTH), whole(LAYERS, DIN, TOKENS)],
        out_specs=(
            pl.BlockSpec((1, WIDTH, FEAT), lambda k: (k, 0, 0)),
            pl.BlockSpec((1, DIN, WIDTH), lambda k: (jnp.minimum(k, LAYERS - 1), 0, 0)),
            whole(LAYERS, WIDTH),
        ),
        name="weight_grads",
    )(act, res, pg, xt)


def body(inputs, encoder, enc_bias, decoder, dec_bias, targets, top_index):
    act, res, pg, xt = main_call(
        inputs.reshape(TOKENS * LAYERS, DIN), encoder, enc_bias, decoder[0], dec_bias[0],
        targets[0], jnp.transpose(top_index, (1, 2, 0)))
    dg, eg, bg = grad_call(act, res, pg, xt)
    return dg[None], eg, bg


def solution(mesh):
    return jax.shard_map(
        body,
        mesh=mesh,
        in_specs=(
            P(None, None, "layer"),
            P(None, "layer", "lat"),
            P(None, "lat"),
            P("layer", None, "lat", None),
            P("layer", None, None),
            P("layer", None, None, None),
            P(),
        ),
        out_specs=(P("layer", None, "lat", None), P(None, "layer", "lat"), P(None, "lat")),
        check_vma=False,
    )
```

```python
import jax
import jax.numpy as jnp
from jax import lax
from jax.experimental import pallas as pl
from jax.experimental.pallas import tpu as pltpu
from jax.sharding import PartitionSpec as P

MESH = pl.DeviceIdType.MESH
F32 = jnp.float32
BF16 = jnp.bfloat16
I32 = jnp.int32

TOKENS, LAYERS, TOPK, WIDTH, DIN, FEAT, BLOCKS, SLOTS = 128, 4, 64, 1024, 128, 256, 5, 8
WIRE = F32


def pick(values, lanes):
    return jnp.take_along_axis(values, lanes, axis=1, mode="promise_in_bounds")


def main_kernel(x_hbm, enc_hbm, bias_hbm, dec_hbm, dbias_hbm, tgt_hbm, idx_hbm,
                act_ref, res_ref, pg_ref, xt_ref,
                x_v, enc_v, bias_v, dec_v, dbias_v, tgt_v, idx_v, load_sem,
                xf, dense, inv, code_v, low_v, high_v, rec, goal,
                ybuf1, zbuf1, ybuf2, zbuf2, rs_src, rs_buf, hbuf, abuf, val_v,
                y1_s, y1_r, z1_s, z1_r, y2_s, y2_r, z2_s, z2_r,
                rs_s, rs_r, h_s, h_r, ag_s, ag_r):
    r = lax.axis_index("layer")
    j = lax.axis_index("lat")
    y = lax.rem(r, 4)
    zl = lax.div(r, 4)
    q = lax.rem(j, 8)
    zh = lax.div(j, 8)
    g = lax.div(r, 8)

    loads = [
        pltpu.make_async_copy(idx_hbm, idx_v, load_sem.at[0]),
        pltpu.make_async_copy(x_hbm, x_v, load_sem.at[1]),
        pltpu.make_async_copy(enc_hbm, enc_v, load_sem.at[2]),
        pltpu.make_async_copy(bias_hbm, bias_v, load_sem.at[3]),
        pltpu.make_async_copy(dec_hbm, dec_v, load_sem.at[4]),
        pltpu.make_async_copy(dbias_hbm, dbias_v, load_sem.at[5]),
        pltpu.make_async_copy(tgt_hbm.at[pl.ds(q * 16, 16)], tgt_v, load_sem.at[6]),
    ]
    for n in (0, 1, 2, 3, 5, 6):
        loads[n].start()

    def ypeer(i):
        return {"layer": zl * 4 + lax.rem(y + i, 4)}

    def zpeer(i):
        return {"layer": lax.rem(zl + i, 4) * 4 + y}

    def qpeer(i):
        return {"lat": zh * 8 + lax.rem(q + i, 8)}

    hpeer = {"lat": (1 - zh) * 8 + q}

    barrier = pltpu.get_barrier_semaphore()
    for i in range(1, 4):
        pl.semaphore_signal(barrier, inc=1, device_id=ypeer(i), device_id_type=MESH)
        pl.semaphore_signal(barrier, inc=1, device_id=zpeer(i), device_id_type=MESH)
    for i in range(1, 8):
        pl.semaphore_signal(barrier, inc=1, device_id=qpeer(i), device_id_type=MESH)
    pl.semaphore_signal(barrier, inc=1, device_id=hpeer, device_id_type=MESH)

    lane = lax.broadcasted_iota(I32, (32, 128), 1)
    quarter = lax.shift_right_logical(lane, 5)

    loads[0].wait()
    tri = (lax.broadcasted_iota(I32, (TOPK, TOPK), 1)
           < lax.broadcasted_iota(I32, (TOPK, TOPK), 0)).astype(F32).astype(BF16)
    sub8 = lax.broadcasted_iota(I32, (SLOTS, 128), 0)
    packs = []
    for l in range(LAYERS):
        local = idx_v[l] - j * WIDTH
        inside = (local >= 0) & (local < WIDTH)
        rank = jnp.dot(tri, inside.astype(F32).astype(BF16), preferred_element_type=F32)
        rank = jnp.where(inside, rank, -1.0)
        value = (local + (l * WIDTH + 1)).astype(F32)
        slot_rows = jnp.zeros((SLOTS, 128), F32)
        for s in range(SLOTS):
            row = jnp.sum(jnp.where(rank == float(s), value, 0.0), axis=0, keepdims=True)
            slot_rows = jnp.where(sub8 == s, row, slot_rows)
        packs.append(slot_rows)
    packed = jnp.concatenate(packs * 4, axis=0)
    code = jnp.transpose(packed).astype(I32) - 1
    code_v[...] = code
    low_v[...] = code & 127
    high_v[...] = lax.shift_right_arithmetic(code, 7)

    loads[1].wait()
    loads[2].wait()
    loads[3].wait()
    xf[...] = x_v[...].astype(F32)
    loads[4].start()
    own = jnp.where(r == 0, 1.0, 0.0)
    for l in range(LAYERS):
        x_l = xf[pl.ds(l, TOKENS, stride=4), :]
        dense[l] = (jnp.dot(x_l.astype(BF16), enc_v[l], preferred_element_type=F32)
                    + bias_v[pl.ds(l, 1), :] * own)

    def gather():
        def step(tq, out):
            rows = pl.ds(pl.multiple_of(tq * 32, 32), 32)
            low = low_v[rows, :]
            high = high_v[rows, :]
            got = jnp.zeros((32, 128), F32)
            for b in range(32):
                block = dense[b // 8, rows, pl.ds((b % 8) * 128, 128)]
                got = jnp.where(high == b, pick(block, low), got)
            return jnp.where(quarter == tq, got, out)

        return lax.fori_loop(0, 4, step, jnp.zeros((32, 128), F32))

    def scatter(out_ref):
        def step(tq, carry):
            rows = pl.ds(pl.multiple_of(tq * 32, 32), 32)
            values = val_v[...]
            for b in range(32):
                cols = pl.ds((b % 8) * 128, 128)
                where = inv[b // 8, rows, cols]
                got = jnp.where(where >= 0, pick(values, where & 127), 0.0)
                out_ref[b // 8, rows, cols] = got.astype(BF16)
            return carry

        lax.fori_loop(0, 4, step, 0)

    def send(src, dst, s_sem, r_sem, peer):
        copy = pltpu.make_async_remote_copy(
            src_ref=src, dst_ref=dst, send_sem=s_sem, recv_sem=r_sem,
            device_id=peer, device_id_type=MESH)
        copy.start()
        return copy

    def exchange(buf, me, n, peer, s_sem, r_sem, between=None):
        sends = [send(buf.at[me], buf.at[me], s_sem.at[i], r_sem.at[me], peer(i))
                 for i in range(n - 1, 0, -1)]
        if between is not None:
            between()
        for i in range(1, n):
            other = lax.rem(me + i, n)
            pltpu.make_async_remote_copy(
                src_ref=buf.at[other], dst_ref=buf.at[other], send_sem=s_sem.at[i],
                recv_sem=r_sem.at[other], device_id=peer(i), device_id_type=MESH).wait_recv()
        for copy in sends:
            copy.wait_send()

    def total(buf, n):
        acc = buf[0].astype(F32)
        for i in range(1, n):
            acc = acc + buf[i].astype(F32)
        return acc

    def build_inverse():
        def step(c, carry):
            rows = pl.ds(pl.multiple_of(c * 16, 16), 16)
            base = lax.div(c, 2) * 32
            lane16 = lax.broadcasted_iota(I32, (16, 128), 1)
            code_rows = code_v[rows, :]
            for l in range(LAYERS):
                found = [jnp.full((16, 128), -1, I32) for h in range(8)]
                for s in range(SLOTS):
                    col = l * SLOTS + s
                    at = jnp.broadcast_to(code_rows[:, col:col + 1], (16, 128)) - l * WIDTH
                    for h in range(8):
                        found[h] = jnp.where(at == lane16 + h * 128, base + col, found[h])
                for h in range(8):
                    inv[l, rows, pl.ds(h * 128, 128)] = found[h]
            return carry

        lax.fori_loop(0, 8, step, 0)
        loads[5].wait()
        loads[6].wait()
        goal_all = tgt_v[...].astype(F32)
        for c in range(2):
            goal[c] = goal_all[:, c, :]

    def transpose_inputs():
        for l in range(LAYERS):
            xt_ref[l] = jnp.transpose(xf[pl.ds(l, TOKENS, stride=4), :]).astype(BF16)

    ybuf1[y] = gather().astype(WIRE)
    pl.semaphore_wait(barrier, 14)
    exchange(ybuf1, y, 4, ypeer, y1_s, y1_r, between=build_inverse)
    zbuf1[zl] = total(ybuf1, 4).astype(WIRE)
    exchange(zbuf1, zl, 4, zpeer, z1_s, z1_r, between=transpose_inputs)
    val_v[...] = total(zbuf1, 4).astype(BF16).astype(F32)
    scatter(act_ref)

    loads[4].wait()
    first = jnp.where(g == 1, 0, 1)

    def source_of(k):
        return jnp.where(k <= g, k, k - g - 1)

    def slot_of(k):
        return jnp.where(k <= g, 0, 1)

    def rebuild(k):
        return jnp.dot(act_ref[source_of(k)], dec_v[k], preferred_element_type=F32)

    rec[0] = rebuild(0)
    rec[1] = rebuild(2) + rebuild(3) + rebuild(4)
    rec[first] = rec[first] + rebuild(1)
    for c in range(2):
        rs_src[:, c] = rec[c].reshape(8, 16, FEAT).astype(BF16)
    rs_buf[q] = rs_src[q]
    sends = []
    for i in (4, 3, 5, 2, 6, 1, 7):
        other = lax.rem(q + i, 8)
        sends.append(send(rs_src.at[other], rs_buf.at[q], rs_s.at[i], rs_r.at[q], qpeer(i)))
    dense[...] = jnp.zeros_like(dense)
    for i in range(1, 8):
        other = lax.rem(q + i, 8)
        pltpu.make_async_remote_copy(
            src_ref=rs_buf.at[other], dst_ref=rs_buf.at[other], send_sem=rs_s.at[i],
            recv_sem=rs_r.at[other], device_id=qpeer(i), device_id_type=MESH).wait_recv()
    for copy in sends:
        copy.wait_send()
    hbuf[zh] = total(rs_buf, 8).astype(hbuf.dtype)
    copy = send(hbuf.at[zh], hbuf.at[zh], h_s, h_r.at[zh], hpeer)
    pltpu.make_async_remote_copy(
        src_ref=hbuf.at[1 - zh], dst_ref=hbuf.at[1 - zh], send_sem=h_s,
        recv_sem=h_r.at[1 - zh], device_id=hpeer, device_id_type=MESH).wait_recv()
    copy.wait_send()
    rebuilt = total(hbuf, 2)
    for c in range(2):
        abuf[q, c] = (rebuilt[c] + dbias_v[pl.ds(c, 1), :] - goal[c]).astype(BF16)
    exchange(abuf, q, 8, qpeer, ag_s, ag_r)

    for k in range(BLOCKS):
        residue = abuf[:, slot_of(k)].reshape(TOKENS, FEAT)
        dense[source_of(k)] = dense[source_of(k)] + lax.dot_general(
            residue, dec_v[k], (((1,), (1,)), ((), ())), preferred_element_type=F32)
    ybuf2[y] = gather().astype(WIRE)
    def keep_residue():
        res_ref[...] = abuf[...]

    exchange(ybuf2, y, 4, ypeer, y2_s, y2_r, between=keep_residue)
    zbuf2[zl] = total(ybuf2, 4).astype(WIRE)
    exchange(zbuf2, zl, 4, zpeer, z2_s, z2_r)
    val_v[...] = total(zbuf2, 4).astype(BF16).astype(F32)
    scatter(pg_ref)


def main_call(x, enc, bias, dec, dbias, tgt, idx):
    dma = pltpu.SemaphoreType.DMA
    vmem = pltpu.VMEM
    return pl.pallas_call(
        main_kernel,
        out_shape=(
            jax.ShapeDtypeStruct((LAYERS, TOKENS, WIDTH), BF16),
            jax.ShapeDtypeStruct((8, 2, 16, FEAT), BF16),
            jax.ShapeDtypeStruct((LAYERS, TOKENS, WIDTH), BF16),
            jax.ShapeDtypeStruct((LAYERS, DIN, TOKENS), BF16),
        ),
        in_specs=[pl.BlockSpec(memory_space=pltpu.HBM)] * 7,
        out_specs=(pl.BlockSpec(memory_space=pltpu.VMEM),) * 4,
        scratch_shapes=[
            vmem((TOKENS * LAYERS, DIN), BF16),
            vmem((LAYERS, DIN, WIDTH), BF16),
            vmem((LAYERS, WIDTH), F32),
            vmem((BLOCKS, WIDTH, FEAT), BF16),
            vmem((2, FEAT), F32),
            vmem((16, 2, FEAT), BF16),
            vmem((LAYERS, TOPK, TOKENS), I32),
            dma((7,)),
            vmem((TOKENS * LAYERS, DIN), F32),
            vmem((LAYERS, TOKENS, WIDTH), F32),
            vmem((LAYERS, TOKENS, WIDTH), I32),
            vmem((TOKENS, 128), I32),
            vmem((TOKENS, 128), I32),
            vmem((TOKENS, 128), I32),
            vmem((2, TOKENS, FEAT), F32),
            vmem((2, 16, FEAT), F32),
            vmem((4, 32, 128), WIRE),
            vmem((4, 32, 128), WIRE),
            vmem((4, 32, 128), WIRE),
            vmem((4, 32, 128), WIRE),
            vmem((8, 2, 16, FEAT), BF16),
            vmem((8, 2, 16, FEAT), BF16),
            vmem((2, 2, 16, FEAT), WIRE),
            vmem((8, 2, 16, FEAT), BF16),
            vmem((32, 128), F32),
            dma((4,)), dma((4,)), dma((4,)), dma((4,)),
            dma((4,)), dma((4,)), dma((4,)), dma((4,)),
            dma((8,)), dma((8,)), dma, dma((2,)), dma((8,)), dma((8,)),
        ],
        compiler_params=pltpu.CompilerParams(collective_id=0, has_side_effects=True,
                                             vmem_limit_bytes=24 * 2**20),
        name="transcoder",
    )(*[pltpu.with_memory_space_constraint(v, pltpu.HBM) for v in (x, enc, bias, dec, dbias, tgt, idx)])


def grad_kernel(act_ref, res_ref, pg_ref, xt_ref, dg_hbm, eg_hbm, bg_ref, dg_v, eg_v, sem):
    g = lax.div(lax.axis_index("layer"), 8)
    copies = []
    for k in range(LAYERS):
        eg_v[k] = jnp.dot(xt_ref[k], pg_ref[k], preferred_element_type=F32)
        copies.append(pltpu.make_async_copy(eg_v.at[k], eg_hbm.at[k], sem.at[BLOCKS + k]))
        copies[-1].start()
    for k in range(BLOCKS):
        source = jnp.where(k <= g, k, k - g - 1)
        slot = jnp.where(k <= g, 0, 1)
        residue = res_ref[:, slot].reshape(TOKENS, FEAT)
        dg_v[k] = lax.dot_general(act_ref[source], residue, (((0,), (0,)), ((), ())),
                                  preferred_element_type=F32)
        copies.append(pltpu.make_async_copy(dg_v.at[k], dg_hbm.at[k], sem.at[k]))
        copies[-1].start()
    for k in range(LAYERS):
        bg_ref[pl.ds(k, 1), :] = jnp.dot(jnp.ones((8, TOKENS), BF16), pg_ref[k],
                                         preferred_element_type=F32)[0:1]
    for copy in copies:
        copy.wait()


def grad_call(act, res, pg, xt):
    vmem = pltpu.VMEM
    return pl.pallas_call(
        grad_kernel,
        out_shape=(
            jax.ShapeDtypeStruct((BLOCKS, WIDTH, FEAT), F32),
            jax.ShapeDtypeStruct((LAYERS, DIN, WIDTH), F32),
            jax.ShapeDtypeStruct((LAYERS, WIDTH), F32),
        ),
        in_specs=[pl.BlockSpec(memory_space=vmem)] * 4,
        out_specs=(pl.BlockSpec(memory_space=pl.ANY), pl.BlockSpec(memory_space=pl.ANY),
                   pl.BlockSpec(memory_space=vmem)),
        scratch_shapes=[vmem((BLOCKS, WIDTH, FEAT), F32), vmem((LAYERS, DIN, WIDTH), F32),
                        pltpu.SemaphoreType.DMA((BLOCKS + LAYERS,))],
        compiler_params=pltpu.CompilerParams(vmem_limit_bytes=24 * 2**20),
        name="weight_grads",
    )(act, res, pg, xt)


def body(inputs, encoder, enc_bias, decoder, dec_bias, targets, top_index):
    act, res, pg, xt = main_call(
        inputs.reshape(TOKENS * LAYERS, DIN), encoder, enc_bias, decoder[0], dec_bias[0],
        targets[0], jnp.transpose(top_index, (1, 2, 0)))
    dg, eg, bg = grad_call(act, res, pg, xt)
    return dg[None], eg, bg


def solution(mesh):
    return jax.shard_map(
        body,
        mesh=mesh,
        in_specs=(
            P(None, None, "layer"),
            P(None, "layer", "lat"),
            P(None, "lat"),
            P("layer", None, "lat", None),
            P("layer", None, None),
            P("layer", None, None, None),
            P(),
        ),
        out_specs=(P("layer", None, "lat", None), P(None, "layer", "lat"), P(None, "lat")),
        check_vma=False,
    )
```

```python
import jax
import jax.numpy as jnp
from jax import lax
from jax.experimental import pallas as pl
from jax.experimental.pallas import tpu as pltpu
from jax.sharding import PartitionSpec as P

MESH = pl.DeviceIdType.MESH
F32 = jnp.float32
BF16 = jnp.bfloat16
I32 = jnp.int32

TOKENS, LAYERS, TOPK, WIDTH, DIN, FEAT, BLOCKS, SLOTS = 128, 4, 64, 1024, 128, 256, 5, 8
WIRE = BF16


def pick(values, lanes):
    return jnp.take_along_axis(values, lanes, axis=1, mode="promise_in_bounds")


def main_kernel(x_hbm, enc_hbm, bias_hbm, dec_hbm, dbias_hbm, tgt_hbm, idx_hbm,
                act_ref, res_ref, pg_ref, xt_ref,
                x_v, enc_v, bias_v, dec_v, dbias_v, tgt_v, idx_v, load_sem,
                xf, dense, inv, code_v, low_v, high_v, rec, goal,
                lbuf1, lbuf2, rs_src, rs_buf, hbuf, abuf, val_v,
                l1_s, l1_r, l2_s, l2_r,
                rs_s, rs_r, h_s, h_r, ag_s, ag_r):
    r = lax.axis_index("layer")
    j = lax.axis_index("lat")
    q = lax.rem(j, 8)
    zh = lax.div(j, 8)
    g = lax.div(r, 8)

    loads = [
        pltpu.make_async_copy(idx_hbm, idx_v, load_sem.at[0]),
        pltpu.make_async_copy(x_hbm, x_v, load_sem.at[1]),
        pltpu.make_async_copy(enc_hbm, enc_v, load_sem.at[2]),
        pltpu.make_async_copy(bias_hbm, bias_v, load_sem.at[3]),
        pltpu.make_async_copy(dec_hbm, dec_v, load_sem.at[4]),
        pltpu.make_async_copy(dbias_hbm, dbias_v, load_sem.at[5]),
        pltpu.make_async_copy(tgt_hbm.at[pl.ds(q * 16, 16)], tgt_v, load_sem.at[6]),
    ]
    for n in (0, 1, 2, 3, 5, 6):
        loads[n].start()

    def lpeer(i):
        return {"layer": lax.rem(r + i, 16)}

    def qpeer(i):
        return {"lat": zh * 8 + lax.rem(q + i, 8)}

    hpeer = {"lat": (1 - zh) * 8 + q}

    barrier = pltpu.get_barrier_semaphore()
    for i in range(1, 16):
        pl.semaphore_signal(barrier, inc=1, device_id=lpeer(i), device_id_type=MESH)
    for i in range(1, 8):
        pl.semaphore_signal(barrier, inc=1, device_id=qpeer(i), device_id_type=MESH)
    pl.semaphore_signal(barrier, inc=1, device_id=hpeer, device_id_type=MESH)

    lane = lax.broadcasted_iota(I32, (32, 128), 1)
    quarter = lax.shift_right_logical(lane, 5)

    loads[0].wait()
    tri = (lax.broadcasted_iota(I32, (TOPK, TOPK), 1)
           < lax.broadcasted_iota(I32, (TOPK, TOPK), 0)).astype(F32).astype(BF16)
    sub8 = lax.broadcasted_iota(I32, (SLOTS, 128), 0)
    packs = []
    for l in range(LAYERS):
        local = idx_v[l] - j * WIDTH
        inside = (local >= 0) & (local < WIDTH)
        rank = jnp.dot(tri, inside.astype(F32).astype(BF16), preferred_element_type=F32)
        rank = jnp.where(inside, rank, -1.0)
        value = (local + (l * WIDTH + 1)).astype(F32)
        slot_rows = jnp.zeros((SLOTS, 128), F32)
        for s in range(SLOTS):
            row = jnp.sum(jnp.where(rank == float(s), value, 0.0), axis=0, keepdims=True)
            slot_rows = jnp.where(sub8 == s, row, slot_rows)
        packs.append(slot_rows)
    packed = jnp.concatenate(packs * 4, axis=0)
    code = jnp.transpose(packed).astype(I32) - 1
    code_v[...] = code
    low_v[...] = code & 127
    high_v[...] = lax.shift_right_arithmetic(code, 7)

    loads[1].wait()
    loads[2].wait()
    loads[3].wait()
    xf[...] = x_v[...].astype(F32)
    loads[4].start()
    own = jnp.where(r == 0, 1.0, 0.0)
    for l in range(LAYERS):
        x_l = xf[pl.ds(l, TOKENS, stride=4), :]
        dense[l] = (jnp.dot(x_l.astype(BF16), enc_v[l], preferred_element_type=F32)
                    + bias_v[pl.ds(l, 1), :] * own)

    def gather():
        def step(tq, out):
            rows = pl.ds(pl.multiple_of(tq * 32, 32), 32)
            low = low_v[rows, :]
            high = high_v[rows, :]
            got = jnp.zeros((32, 128), F32)
            for b in range(32):
                block = dense[b // 8, rows, pl.ds((b % 8) * 128, 128)]
                got = jnp.where(high == b, pick(block, low), got)
            return jnp.where(quarter == tq, got, out)

        return lax.fori_loop(0, 4, step, jnp.zeros((32, 128), F32))

    def scatter(out_ref):
        def step(tq, carry):
            rows = pl.ds(pl.multiple_of(tq * 32, 32), 32)
            values = val_v[...]
            for b in range(32):
                cols = pl.ds((b % 8) * 128, 128)
                where = inv[b // 8, rows, cols]
                got = jnp.where(where >= 0, pick(values, where & 127), 0.0)
                out_ref[b // 8, rows, cols] = got.astype(BF16)
            return carry

        lax.fori_loop(0, 4, step, 0)

    def send(src, dst, s_sem, r_sem, peer):
        copy = pltpu.make_async_remote_copy(
            src_ref=src, dst_ref=dst, send_sem=s_sem, recv_sem=r_sem,
            device_id=peer, device_id_type=MESH)
        copy.start()
        return copy

    def exchange(buf, me, n, peer, s_sem, r_sem, between=None):
        sends = [send(buf.at[me], buf.at[me], s_sem.at[i], r_sem.at[me], peer(i))
                 for i in range(n - 1, 0, -1)]
        if between is not None:
            between()
        for i in range(1, n):
            other = lax.rem(me + i, n)
            pltpu.make_async_remote_copy(
                src_ref=buf.at[other], dst_ref=buf.at[other], send_sem=s_sem.at[i],
                recv_sem=r_sem.at[other], device_id=peer(i), device_id_type=MESH).wait_recv()
        for copy in sends:
            copy.wait_send()

    def total(buf, n):
        acc = buf[0].astype(F32)
        for i in range(1, n):
            acc = acc + buf[i].astype(F32)
        return acc

    def build_inverse():
        def step(c, carry):
            rows = pl.ds(pl.multiple_of(c * 16, 16), 16)
            base = lax.div(c, 2) * 32
            lane16 = lax.broadcasted_iota(I32, (16, 128), 1)
            code_rows = code_v[rows, :]
            for l in range(LAYERS):
                found = [jnp.full((16, 128), -1, I32) for h in range(8)]
                for s in range(SLOTS):
                    col = l * SLOTS + s
                    at = jnp.broadcast_to(code_rows[:, col:col + 1], (16, 128)) - l * WIDTH
                    for h in range(8):
                        found[h] = jnp.where(at == lane16 + h * 128, base + col, found[h])
                for h in range(8):
                    inv[l, rows, pl.ds(h * 128, 128)] = found[h]
            return carry

        lax.fori_loop(0, 8, step, 0)
        loads[5].wait()
        loads[6].wait()
        goal_all = tgt_v[...].astype(F32)
        for c in range(2):
            goal[c] = goal_all[:, c, :]

    def transpose_inputs():
        for l in range(LAYERS):
            xt_ref[l] = jnp.transpose(xf[pl.ds(l, TOKENS, stride=4), :]).astype(BF16)

    lbuf1[r] = gather().astype(WIRE)
    pl.semaphore_wait(barrier, 23)

    def hidden():
        build_inverse()
        transpose_inputs()

    exchange(lbuf1, r, 16, lpeer, l1_s, l1_r, between=hidden)
    val_v[...] = total(lbuf1, 16).astype(BF16).astype(F32)
    scatter(act_ref)

    loads[4].wait()
    first = jnp.where(g == 1, 0, 1)

    def source_of(k):
        return jnp.where(k <= g, k, k - g - 1)

    def slot_of(k):
        return jnp.where(k <= g, 0, 1)

    def rebuild(k):
        return jnp.dot(act_ref[source_of(k)], dec_v[k], preferred_element_type=F32)

    rec[0] = rebuild(0)
    rec[1] = rebuild(2) + rebuild(3) + rebuild(4)
    rec[first] = rec[first] + rebuild(1)
    for c in range(2):
        rs_src[:, c] = rec[c].reshape(8, 16, FEAT).astype(BF16)
    rs_buf[q] = rs_src[q]
    sends = []
    for i in (4, 3, 5, 2, 6, 1, 7):
        other = lax.rem(q + i, 8)
        sends.append(send(rs_src.at[other], rs_buf.at[q], rs_s.at[i], rs_r.at[q], qpeer(i)))
    dense[...] = jnp.zeros_like(dense)
    for i in range(1, 8):
        other = lax.rem(q + i, 8)
        pltpu.make_async_remote_copy(
            src_ref=rs_buf.at[other], dst_ref=rs_buf.at[other], send_sem=rs_s.at[i],
            recv_sem=rs_r.at[other], device_id=qpeer(i), device_id_type=MESH).wait_recv()
    for copy in sends:
        copy.wait_send()
    hbuf[zh] = total(rs_buf, 8).astype(hbuf.dtype)
    copy = send(hbuf.at[zh], hbuf.at[zh], h_s, h_r.at[zh], hpeer)
    pltpu.make_async_remote_copy(
        src_ref=hbuf.at[1 - zh], dst_ref=hbuf.at[1 - zh], send_sem=h_s,
        recv_sem=h_r.at[1 - zh], device_id=hpeer, device_id_type=MESH).wait_recv()
    copy.wait_send()
    rebuilt = total(hbuf, 2)
    for c in range(2):
        abuf[q, c] = (rebuilt[c] + dbias_v[pl.ds(c, 1), :] - goal[c]).astype(BF16)
    exchange(abuf, q, 8, qpeer, ag_s, ag_r)

    for k in range(BLOCKS):
        residue = abuf[:, slot_of(k)].reshape(TOKENS, FEAT)
        dense[source_of(k)] = dense[source_of(k)] + lax.dot_general(
            residue, dec_v[k], (((1,), (1,)), ((), ())), preferred_element_type=F32)
    lbuf2[r] = gather().astype(WIRE)

    def keep_residue():
        res_ref[...] = abuf[...]

    exchange(lbuf2, r, 16, lpeer, l2_s, l2_r, between=keep_residue)
    val_v[...] = total(lbuf2, 16).astype(BF16).astype(F32)
    scatter(pg_ref)


def main_call(x, enc, bias, dec, dbias, tgt, idx):
    dma = pltpu.SemaphoreType.DMA
    vmem = pltpu.VMEM
    return pl.pallas_call(
        main_kernel,
        out_shape=(
            jax.ShapeDtypeStruct((LAYERS, TOKENS, WIDTH), BF16),
            jax.ShapeDtypeStruct((8, 2, 16, FEAT), BF16),
            jax.ShapeDtypeStruct((LAYERS, TOKENS, WIDTH), BF16),
            jax.ShapeDtypeStruct((LAYERS, DIN, TOKENS), BF16),
        ),
        in_specs=[pl.BlockSpec(memory_space=pltpu.HBM)] * 7,
        out_specs=(pl.BlockSpec(memory_space=pltpu.VMEM),) * 4,
        scratch_shapes=[
            vmem((TOKENS * LAYERS, DIN), BF16),
            vmem((LAYERS, DIN, WIDTH), BF16),
            vmem((LAYERS, WIDTH), F32),
            vmem((BLOCKS, WIDTH, FEAT), BF16),
            vmem((2, FEAT), F32),
            vmem((16, 2, FEAT), BF16),
            vmem((LAYERS, TOPK, TOKENS), I32),
            dma((7,)),
            vmem((TOKENS * LAYERS, DIN), F32),
            vmem((LAYERS, TOKENS, WIDTH), F32),
            vmem((LAYERS, TOKENS, WIDTH), I32),
            vmem((TOKENS, 128), I32),
            vmem((TOKENS, 128), I32),
            vmem((TOKENS, 128), I32),
            vmem((2, TOKENS, FEAT), F32),
            vmem((2, 16, FEAT), F32),
            vmem((16, 32, 128), WIRE),
            vmem((16, 32, 128), WIRE),
            vmem((8, 2, 16, FEAT), BF16),
            vmem((8, 2, 16, FEAT), BF16),
            vmem((2, 2, 16, FEAT), WIRE),
            vmem((8, 2, 16, FEAT), BF16),
            vmem((32, 128), F32),
            dma((16,)), dma((16,)), dma((16,)), dma((16,)),
            dma((8,)), dma((8,)), dma, dma((2,)), dma((8,)), dma((8,)),
        ],
        compiler_params=pltpu.CompilerParams(collective_id=0, has_side_effects=True,
                                             vmem_limit_bytes=24 * 2**20),
        name="transcoder",
    )(*[pltpu.with_memory_space_constraint(v, pltpu.HBM) for v in (x, enc, bias, dec, dbias, tgt, idx)])


def grad_kernel(act_ref, res_ref, pg_ref, xt_ref, dg_hbm, eg_hbm, bg_ref, dg_v, eg_v, sem):
    g = lax.div(lax.axis_index("layer"), 8)
    copies = []
    for k in range(LAYERS):
        eg_v[k] = jnp.dot(xt_ref[k], pg_ref[k], preferred_element_type=F32)
        copies.append(pltpu.make_async_copy(eg_v.at[k], eg_hbm.at[k], sem.at[BLOCKS + k]))
        copies[-1].start()
    for k in range(BLOCKS):
        source = jnp.where(k <= g, k, k - g - 1)
        slot = jnp.where(k <= g, 0, 1)
        residue = res_ref[:, slot].reshape(TOKENS, FEAT)
        dg_v[k] = lax.dot_general(act_ref[source], residue, (((0,), (0,)), ((), ())),
                                  preferred_element_type=F32)
        copies.append(pltpu.make_async_copy(dg_v.at[k], dg_hbm.at[k], sem.at[k]))
        copies[-1].start()
    for k in range(LAYERS):
        bg_ref[pl.ds(k, 1), :] = jnp.dot(jnp.ones((8, TOKENS), BF16), pg_ref[k],
                                         preferred_element_type=F32)[0:1]
    for copy in copies:
        copy.wait()


def grad_call(act, res, pg, xt):
    vmem = pltpu.VMEM
    return pl.pallas_call(
        grad_kernel,
        out_shape=(
            jax.ShapeDtypeStruct((BLOCKS, WIDTH, FEAT), F32),
            jax.ShapeDtypeStruct((LAYERS, DIN, WIDTH), F32),
            jax.ShapeDtypeStruct((LAYERS, WIDTH), F32),
        ),
        in_specs=[pl.BlockSpec(memory_space=vmem)] * 4,
        out_specs=(pl.BlockSpec(memory_space=pl.ANY), pl.BlockSpec(memory_space=pl.ANY),
                   pl.BlockSpec(memory_space=vmem)),
        scratch_shapes=[vmem((BLOCKS, WIDTH, FEAT), F32), vmem((LAYERS, DIN, WIDTH), F32),
                        pltpu.SemaphoreType.DMA((BLOCKS + LAYERS,))],
        compiler_params=pltpu.CompilerParams(vmem_limit_bytes=24 * 2**20),
        name="weight_grads",
    )(act, res, pg, xt)


def body(inputs, encoder, enc_bias, decoder, dec_bias, targets, top_index):
    act, res, pg, xt = main_call(
        inputs.reshape(TOKENS * LAYERS, DIN), encoder, enc_bias, decoder[0], dec_bias[0],
        targets[0], jnp.transpose(top_index, (1, 2, 0)))
    dg, eg, bg = grad_call(act, res, pg, xt)
    return dg[None], eg, bg


def solution(mesh):
    return jax.shard_map(
        body,
        mesh=mesh,
        in_specs=(
            P(None, None, "layer"),
            P(None, "layer", "lat"),
            P(None, "lat"),
            P("layer", None, "lat", None),
            P("layer", None, None),
            P("layer", None, None, None),
            P(),
        ),
        out_specs=(P("layer", None, "lat", None), P(None, "layer", "lat"), P(None, "lat")),
        check_vma=False,
    )
```

```python
import jax
import jax.numpy as jnp
from jax import lax
from jax.experimental import pallas as pl
from jax.experimental.pallas import tpu as pltpu
from jax.sharding import PartitionSpec as P

MESH = pl.DeviceIdType.MESH
F32 = jnp.float32
BF16 = jnp.bfloat16
I32 = jnp.int32

TOKENS, LAYERS, TOPK, WIDTH, DIN, FEAT, BLOCKS, SLOTS = 128, 4, 64, 1024, 128, 256, 5, 8


def pick(values, lanes):
    return jnp.take_along_axis(values, lanes, axis=1, mode="promise_in_bounds")


def main_kernel(x_hbm, enc_hbm, bias_hbm, dec_hbm, dbias_hbm, tgt_hbm, idx_hbm,
                act_ref, res_ref, pg_ref, xt_ref,
                x_v, enc_v, bias_v, dec_v, dbias_v, tgt_v, idx_v, load_sem,
                xf, dense, inv, code_v, low_v, high_v, hot_a, hot_b, rows_v, val_v, pay_v, goal,
                ybuf, zbuf, lbuf, rs_src, rs_buf, hbuf, abuf,
                y_s, y_r, z_s, z_r, l_s, l_r, rs_s, rs_r, h_s, h_r, ag_s, ag_r):
    r = lax.axis_index("layer")
    j = lax.axis_index("lat")
    y = lax.rem(r, 4)
    zl = lax.div(r, 4)
    q = lax.rem(j, 8)
    zh = lax.div(j, 8)
    g = lax.div(r, 8)

    loads = [
        pltpu.make_async_copy(idx_hbm, idx_v, load_sem.at[0]),
        pltpu.make_async_copy(x_hbm, x_v, load_sem.at[1]),
        pltpu.make_async_copy(enc_hbm, enc_v, load_sem.at[2]),
        pltpu.make_async_copy(bias_hbm, bias_v, load_sem.at[3]),
        pltpu.make_async_copy(dec_hbm, dec_v, load_sem.at[4]),
        pltpu.make_async_copy(dbias_hbm, dbias_v, load_sem.at[5]),
        pltpu.make_async_copy(tgt_hbm.at[pl.ds(q * 16, 16)], tgt_v, load_sem.at[6]),
    ]
    for n in (0, 1, 2, 3, 5, 6):
        loads[n].start()

    def ypeer(i):
        return {"layer": zl * 4 + lax.rem(y + i, 4)}

    def zpeer(i):
        return {"layer": lax.rem(zl + i, 4) * 4 + y}

    def lpeer(i):
        return {"layer": lax.rem(r + i, 16)}

    def qpeer(i):
        return {"lat": zh * 8 + lax.rem(q + i, 8)}

    hpeer = {"lat": (1 - zh) * 8 + q}

    barrier = pltpu.get_barrier_semaphore()
    for i in range(1, 16):
        pl.semaphore_signal(barrier, inc=1, device_id=lpeer(i), device_id_type=MESH)
    for i in range(1, 8):
        pl.semaphore_signal(barrier, inc=1, device_id=qpeer(i), device_id_type=MESH)
    pl.semaphore_signal(barrier, inc=1, device_id=hpeer, device_id_type=MESH)

    lane16 = lax.broadcasted_iota(I32, (16, 128), 1)
    row16 = lax.broadcasted_iota(I32, (16, 128), 0)
    mine = (lane16 & 15) == row16

    loads[0].wait()
    tri = (lax.broadcasted_iota(I32, (TOPK, TOPK), 1)
           < lax.broadcasted_iota(I32, (TOPK, TOPK), 0)).astype(F32).astype(BF16)
    for l in range(LAYERS):
        local = idx_v[l] - j * WIDTH
        inside = (local >= 0) & (local < WIDTH)
        rank = jnp.dot(tri, inside.astype(F32).astype(BF16), preferred_element_type=F32)
        rank = jnp.where(inside, rank, -1.0)
        value = (local + 1).astype(F32)
        slots = []
        for s in range(SLOTS):
            row = jnp.sum(jnp.where(rank == float(s), value, 0.0), axis=0, keepdims=True)
            slots.append(jnp.broadcast_to(row, (16, 128)))
        code = jnp.transpose(jnp.concatenate(slots, axis=0)).astype(I32) - 1
        code_v[l] = code
        low_v[l] = code & 127
        high_v[l] = lax.shift_right_arithmetic(code, 7)

    loads[1].wait()
    loads[2].wait()
    loads[3].wait()
    loads[4].start()
    xf[...] = x_v[...].astype(F32)
    own = jnp.where(r == 0, 1.0, 0.0)
    for l in range(LAYERS):
        x_l = xf[pl.ds(l, TOKENS, stride=4), :]
        dense[l] = (jnp.dot(x_l.astype(BF16), enc_v[l], preferred_element_type=F32)
                    + bias_v[pl.ds(l, 1), :] * own)

    def gather(l, carry):
        own_lane = (lax.broadcasted_iota(I32, (TOKENS, 128), 1) & 15) == (
            lax.broadcasted_iota(I32, (TOKENS, 128), 0) & 15)
        low = low_v[l]
        high = high_v[l]
        got = jnp.zeros((TOKENS, 128), F32)
        for h in range(8):
            block = dense[l, :, pl.ds(h * 128, 128)]
            got = jnp.where(high == h, pick(block, low), got)
        got = jnp.where(own_lane, got, 0.0)
        ybuf[y, pl.ds(pl.multiple_of(l * 8, 8), 8), :] = jnp.sum(
            got.reshape(8, 16, 128), axis=1)
        return carry

    def scatter(out_ref):
        def step(b, carry):
            rows = pl.ds(pl.multiple_of(b * 16, 16), 16)
            for l in range(LAYERS):
                values = jnp.broadcast_to(val_v[pl.ds(l * 8 + b, 1), :], (16, 128))
                for h in range(8):
                    cols = pl.ds(h * 128, 128)
                    where = inv[l, rows, cols]
                    got = jnp.where(where >= 0, pick(values, where & 127), 0.0)
                    out_ref[l, rows, cols] = got.astype(BF16)
            return carry

        lax.fori_loop(0, 8, step, 0)

    def send(src, dst, s_sem, r_sem, peer):
        copy = pltpu.make_async_remote_copy(
            src_ref=src, dst_ref=dst, send_sem=s_sem, recv_sem=r_sem,
            device_id=peer, device_id_type=MESH)
        copy.start()
        return copy

    def arrive(buf, other, s_sem, r_sem, peer):
        pltpu.make_async_remote_copy(
            src_ref=buf.at[other], dst_ref=buf.at[other], send_sem=s_sem,
            recv_sem=r_sem, device_id=peer, device_id_type=MESH).wait_recv()

    def exchange(buf, me, n, peer, s_sem, r_sem, between=None):
        sends = [send(buf.at[me], buf.at[me], s_sem.at[i], r_sem.at[me], peer(i))
                 for i in range(n - 1, 0, -1)]
        if between is not None:
            between()
        for i in range(1, n):
            other = lax.rem(me + i, n)
            arrive(buf, other, s_sem.at[i], r_sem.at[other], peer(i))
        for copy in sends:
            copy.wait_send()

    def total(buf, n):
        acc = buf[0].astype(F32)
        for i in range(1, n):
            acc = acc + buf[i].astype(F32)
        return acc

    def source_of(k):
        return jnp.where(k <= g, k, k - g - 1)

    def gather_decoder(begin, end):

        def build(hot, b):
            tokens = pl.ds(pl.multiple_of(b * 16, 16), 16)
            for l in range(LAYERS):
                code = code_v[l, tokens, :]
                for s in range(SLOTS):
                    at = jnp.broadcast_to(code[:, s * 16:s * 16 + 1], (16, 128))
                    for h in range(8):
                        hot[l, pl.ds(s * 16, 16), pl.ds(h * 128, 128)] = jnp.where(
                            at == lane16 + h * 128, 1.0, 0.0).astype(BF16)

        def multiply(hot, b):
            for k in range(BLOCKS):
                rows_v[b, pl.ds(k * 128, 128), :] = jnp.dot(
                    hot[source_of(k)], dec_v[k], preferred_element_type=F32).astype(BF16)

        def step(n, carry):
            build(hot_b, 2 * n + 1)
            multiply(hot_a, 2 * n)
            build(hot_a, jnp.minimum(2 * n + 2, 7))
            multiply(hot_b, 2 * n + 1)
            return carry

        if begin == 0:
            loads[4].wait()
            build(hot_a, 0)
        lax.fori_loop(begin, end, step, 0)

    def build_inverse():
        def step(b, carry):
            tokens = pl.ds(pl.multiple_of(b * 16, 16), 16)
            for l in range(LAYERS):
                code = code_v[l, tokens, :]
                found = [jnp.full((16, 128), -1, I32) for h in range(8)]
                for s in range(SLOTS):
                    at = jnp.broadcast_to(code[:, s * 16:s * 16 + 1], (16, 128))
                    for h in range(8):
                        found[h] = jnp.where(at == lane16 + h * 128, row16 + s * 16, found[h])
                for h in range(8):
                    inv[l, tokens, pl.ds(h * 128, 128)] = found[h]
            return carry

        lax.fori_loop(0, 8, step, 0)

    def prepare():
        gather_decoder(2, 4)
        for l in range(LAYERS):
            xt_ref[l] = jnp.transpose(xf[pl.ds(l, TOKENS, stride=4), :]).astype(BF16)
        loads[5].wait()
        loads[6].wait()
        goal_all = tgt_v[...].astype(F32)
        for c in range(2):
            goal[c] = goal_all[:, c, :]

    lax.fori_loop(0, LAYERS, gather, 0)
    pl.semaphore_wait(barrier, 23)
    exchange(ybuf, y, 4, ypeer, y_s, y_r, between=lambda: gather_decoder(0, 2))
    zbuf[zl] = total(ybuf, 4)
    exchange(zbuf, zl, 4, zpeer, z_s, z_r, between=prepare)
    val_v[...] = total(zbuf, 4).astype(BF16).astype(F32)

    def rebuild(b):
        zero = jnp.zeros((16, 128), F32)
        top, bottom = [], []
        for k in range(BLOCKS):
            row = val_v[pl.ds(source_of(k) * 8 + b, 1), :]
            block = jnp.where(mine, jnp.broadcast_to(row, (16, 128)), 0.0)
            if k == 0:
                top.append(block)
                bottom.append(zero)
            elif k == 1:
                top.append(block * jnp.where(g == 1, 1.0, 0.0))
                bottom.append(block * jnp.where(g == 1, 0.0, 1.0))
            else:
                top.append(zero)
                bottom.append(block)
        left = jnp.concatenate([jnp.concatenate(top, axis=1), jnp.concatenate(bottom, axis=1)],
                               axis=0)
        return jnp.dot(left.astype(BF16), rows_v[b],
                       preferred_element_type=F32).reshape(2, 16, FEAT)

    def give(i):
        other = lax.rem(q + i, 8)
        return send(rs_src.at[other], rs_buf.at[q], rs_s.at[i], rs_r.at[q], qpeer(i))

    order = (4, 3, 5, 2, 6, 1, 7)
    sends = []
    for n, i in enumerate(order):
        b = lax.rem(q + i, 8)
        rs_src[b] = rebuild(b).astype(BF16)
        if n > 0:
            sends.append(give(order[n - 1]))
    rs_buf[q] = rebuild(q).astype(BF16)
    sends.append(give(order[-1]))
    build_inverse()
    for i in range(1, 8):
        other = lax.rem(q + i, 8)
        arrive(rs_buf, other, rs_s.at[i], rs_r.at[other], qpeer(i))
    hbuf[zh] = total(rs_buf, 8)
    copy = send(hbuf.at[zh], hbuf.at[zh], h_s, h_r.at[zh], hpeer)
    scatter(act_ref)
    for other in sends:
        other.wait_send()
    arrive(hbuf, 1 - zh, h_s, h_r.at[1 - zh], hpeer)
    copy.wait_send()
    rebuilt = total(hbuf, 2)
    for c in range(2):
        abuf[q, c] = (rebuilt[c] + dbias_v[pl.ds(c, 1), :] - goal[c]).astype(BF16)

    def back(b):
        out = lax.dot_general(abuf[b].reshape(32, FEAT), rows_v[b], (((1,), (1,)), ((), ())),
                              preferred_element_type=F32)

        def part(c, k):
            block = out[c * 16:c * 16 + 16, k * 128:k * 128 + 128]
            return jnp.sum(jnp.where(mine, block, 0.0), axis=0, keepdims=True)

        p0 = part(0, 0)
        p1 = jnp.where(g == 1, part(0, 1), part(1, 1))
        p2, p3, p4 = part(1, 2), part(1, 3), part(1, 4)
        pay_v[pl.ds(b, 1), :] = p0 + jnp.where(g == 1, p2, p1)
        pay_v[pl.ds(8 + b, 1), :] = jnp.where(g == 1, p1 + p3, p2)
        pay_v[pl.ds(16 + b, 1), :] = jnp.where(g == 1, p4, p3)
        pay_v[pl.ds(24 + b, 1), :] = jnp.where(g == 1, jnp.zeros_like(p4), p4)

    sends = [send(abuf.at[q], abuf.at[q], ag_s.at[i], ag_r.at[q], qpeer(i)) for i in order]
    back(q)
    for i in (1, 7, 2, 6, 3, 5, 4):
        other = lax.rem(q + i, 8)
        arrive(abuf, other, ag_s.at[i], ag_r.at[other], qpeer(i))
        back(other)
    for copy in sends:
        copy.wait_send()
    lbuf[r] = pay_v[...].astype(BF16)

    def keep_residue():
        res_ref[...] = abuf[...]

    exchange(lbuf, r, 16, lpeer, l_s, l_r, between=keep_residue)
    val_v[...] = total(lbuf, 16).astype(BF16).astype(F32)
    scatter(pg_ref)


def main_call(x, enc, bias, dec, dbias, tgt, idx):
    dma = pltpu.SemaphoreType.DMA
    vmem = pltpu.VMEM
    return pl.pallas_call(
        main_kernel,
        out_shape=(
            jax.ShapeDtypeStruct((LAYERS, TOKENS, WIDTH), BF16),
            jax.ShapeDtypeStruct((8, 2, 16, FEAT), BF16),
            jax.ShapeDtypeStruct((LAYERS, TOKENS, WIDTH), BF16),
            jax.ShapeDtypeStruct((LAYERS, DIN, TOKENS), BF16),
        ),
        in_specs=[pl.BlockSpec(memory_space=pltpu.HBM)] * 7,
        out_specs=(pl.BlockSpec(memory_space=pltpu.VMEM),) * 4,
        scratch_shapes=[
            vmem((TOKENS * LAYERS, DIN), BF16),
            vmem((LAYERS, DIN, WIDTH), BF16),
            vmem((LAYERS, WIDTH), F32),
            vmem((BLOCKS, WIDTH, FEAT), BF16),
            vmem((2, FEAT), F32),
            vmem((16, 2, FEAT), BF16),
            vmem((LAYERS, TOPK, TOKENS), I32),
            dma((7,)),
            vmem((TOKENS * LAYERS, DIN), F32),
            vmem((LAYERS, TOKENS, WIDTH), F32),
            vmem((LAYERS, TOKENS, WIDTH), I32),
            vmem((LAYERS, TOKENS, 128), I32),
            vmem((LAYERS, TOKENS, 128), I32),
            vmem((LAYERS, TOKENS, 128), I32),
            vmem((LAYERS, 128, WIDTH), BF16),
            vmem((LAYERS, 128, WIDTH), BF16),
            vmem((8, BLOCKS * 128, FEAT), BF16),
            vmem((32, 128), F32),
            vmem((32, 128), F32),
            vmem((2, 16, FEAT), F32),
            vmem((4, 32, 128), F32),
            vmem((4, 32, 128), F32),
            vmem((16, 32, 128), BF16),
            vmem((8, 2, 16, FEAT), BF16),
            vmem((8, 2, 16, FEAT), BF16),
            vmem((2, 2, 16, FEAT), F32),
            vmem((8, 2, 16, FEAT), BF16),
            dma((4,)), dma((4,)), dma((4,)), dma((4,)), dma((16,)), dma((16,)),
            dma((8,)), dma((8,)), dma, dma((2,)), dma((8,)), dma((8,)),
        ],
        compiler_params=pltpu.CompilerParams(collective_id=0, has_side_effects=True,
                                             vmem_limit_bytes=28 * 2**20),
        name="transcoder",
    )(*[pltpu.with_memory_space_constraint(v, pltpu.HBM)
        for v in (x, enc, bias, dec, dbias, tgt, idx)])


def grad_kernel(act_ref, res_ref, pg_ref, xt_ref, dg_hbm, eg_hbm, bg_ref, dg_v, eg_v, sem):
    g = lax.div(lax.axis_index("layer"), 8)
    copies = []
    for k in range(LAYERS):
        eg_v[k] = jnp.dot(xt_ref[k], pg_ref[k], preferred_element_type=F32)
        copies.append(pltpu.make_async_copy(eg_v.at[k], eg_hbm.at[k], sem.at[BLOCKS + k]))
        copies[-1].start()
    for k in range(BLOCKS):
        source = jnp.where(k <= g, k, k - g - 1)
        slot = jnp.where(k <= g, 0, 1)
        residue = res_ref[:, slot].reshape(TOKENS, FEAT)
        dg_v[k] = lax.dot_general(act_ref[source], residue, (((0,), (0,)), ((), ())),
                                  preferred_element_type=F32)
        copies.append(pltpu.make_async_copy(dg_v.at[k], dg_hbm.at[k], sem.at[k]))
        copies[-1].start()
    for k in range(LAYERS):
        bg_ref[pl.ds(k, 1), :] = jnp.dot(jnp.ones((8, TOKENS), BF16), pg_ref[k],
                                         preferred_element_type=F32)[0:1]
    for copy in copies:
        copy.wait()


def grad_call(act, res, pg, xt):
    vmem = pltpu.VMEM
    return pl.pallas_call(
        grad_kernel,
        out_shape=(
            jax.ShapeDtypeStruct((BLOCKS, WIDTH, FEAT), F32),
            jax.ShapeDtypeStruct((LAYERS, DIN, WIDTH), F32),
            jax.ShapeDtypeStruct((LAYERS, WIDTH), F32),
        ),
        in_specs=[pl.BlockSpec(memory_space=vmem)] * 4,
        out_specs=(pl.BlockSpec(memory_space=pl.ANY), pl.BlockSpec(memory_space=pl.ANY),
                   pl.BlockSpec(memory_space=vmem)),
        scratch_shapes=[vmem((BLOCKS, WIDTH, FEAT), F32), vmem((LAYERS, DIN, WIDTH), F32),
                        pltpu.SemaphoreType.DMA((BLOCKS + LAYERS,))],
        compiler_params=pltpu.CompilerParams(vmem_limit_bytes=24 * 2**20),
        name="weight_grads",
    )(act, res, pg, xt)


def body(inputs, encoder, enc_bias, decoder, dec_bias, targets, top_index):
    act, res, pg, xt = main_call(
        inputs.reshape(TOKENS * LAYERS, DIN), encoder, enc_bias, decoder[0], dec_bias[0],
        targets[0], jnp.transpose(top_index, (1, 2, 0)))
    dg, eg, bg = grad_call(act, res, pg, xt)
    return dg[None], eg, bg


def solution(mesh):
    return jax.shard_map(
        body,
        mesh=mesh,
        in_specs=(
            P(None, None, "layer"),
            P(None, "layer", "lat"),
            P(None, "lat"),
            P("layer", None, "lat", None),
            P("layer", None, None),
            P("layer", None, None, None),
            P(),
        ),
        out_specs=(P("layer", None, "lat", None), P(None, "layer", "lat"), P(None, "lat")),
        check_vma=False,
    )
```

```python
import jax
import jax.numpy as jnp
from jax import lax
from jax.experimental import pallas as pl
from jax.experimental.pallas import tpu as pltpu
from jax.sharding import PartitionSpec as P

MESH = pl.DeviceIdType.MESH
F32 = jnp.float32
BF16 = jnp.bfloat16
I32 = jnp.int32

TOKENS, LAYERS, TOPK, WIDTH, DIN, FEAT, BLOCKS, SLOTS = 128, 4, 64, 1024, 128, 256, 5, 8


def pick(values, lanes):
    return jnp.take_along_axis(values, lanes, axis=1, mode="promise_in_bounds")


def scatter(out_ref, values_ref, inv_ref, l, b):
    rows = pl.ds(pl.multiple_of(b * 16, 16), 16)
    values = jnp.broadcast_to(values_ref[pl.ds(l * 8 + b, 1), :], (16, 128))
    for h in range(8):
        cols = pl.ds(h * 128, 128)
        where = inv_ref[l, rows, cols]
        got = jnp.where(where >= 0, pick(values, where & 127), 0.0)
        out_ref[l, rows, cols] = got.astype(BF16)


def main_kernel(x_hbm, enc_hbm, bias_hbm, dec_hbm, dbias_hbm, tgt_hbm, idx_hbm,
                act_ref, res_ref, pick_ref, inv, xt_ref,
                x_v, enc_v, bias_v, dec_v, dbias_v, tgt_v, idx_v, load_sem,
                xf, dense, code_v, low_v, high_v, hot_a, hot_b, rows_v, val_v, pay_v, goal,
                ybuf, zbuf, lbuf, rs_src, rs_buf, hbuf, abuf,
                y_s, y_r, z_s, z_r, l_s, l_r, rs_s, rs_r, h_s, h_r, ag_s, ag_r):
    r = lax.axis_index("layer")
    j = lax.axis_index("lat")
    y = lax.rem(r, 4)
    zl = lax.div(r, 4)
    q = lax.rem(j, 8)
    zh = lax.div(j, 8)
    g = lax.div(r, 8)

    loads = [
        pltpu.make_async_copy(idx_hbm, idx_v, load_sem.at[0]),
        pltpu.make_async_copy(x_hbm, x_v, load_sem.at[1]),
        pltpu.make_async_copy(enc_hbm, enc_v, load_sem.at[2]),
        pltpu.make_async_copy(bias_hbm, bias_v, load_sem.at[3]),
        pltpu.make_async_copy(dec_hbm, dec_v, load_sem.at[4]),
        pltpu.make_async_copy(dbias_hbm, dbias_v, load_sem.at[5]),
        pltpu.make_async_copy(tgt_hbm.at[pl.ds(q * 16, 16)], tgt_v, load_sem.at[6]),
    ]
    for n in (0, 1, 2, 3, 5, 6):
        loads[n].start()

    def ypeer(i):
        return {"layer": zl * 4 + lax.rem(y + i, 4)}

    def zpeer(i):
        return {"layer": lax.rem(zl + i, 4) * 4 + y}

    def lpeer(i):
        return {"layer": lax.rem(r + i, 16)}

    def qpeer(i):
        return {"lat": zh * 8 + lax.rem(q + i, 8)}

    hpeer = {"lat": (1 - zh) * 8 + q}

    barrier = pltpu.get_barrier_semaphore()
    for i in range(1, 16):
        pl.semaphore_signal(barrier, inc=1, device_id=lpeer(i), device_id_type=MESH)
    for i in range(1, 8):
        pl.semaphore_signal(barrier, inc=1, device_id=qpeer(i), device_id_type=MESH)
    pl.semaphore_signal(barrier, inc=1, device_id=hpeer, device_id_type=MESH)

    lane16 = lax.broadcasted_iota(I32, (16, 128), 1)
    row16 = lax.broadcasted_iota(I32, (16, 128), 0)
    mine = (lane16 & 15) == row16

    loads[0].wait()
    tri = (lax.broadcasted_iota(I32, (TOPK, TOPK), 1)
           < lax.broadcasted_iota(I32, (TOPK, TOPK), 0)).astype(F32).astype(BF16)
    for l in range(LAYERS):
        local = idx_v[l] - j * WIDTH
        inside = (local >= 0) & (local < WIDTH)
        rank = jnp.dot(tri, inside.astype(F32).astype(BF16), preferred_element_type=F32)
        rank = jnp.where(inside, rank, -1.0)
        value = (local + 1).astype(F32)
        slots = []
        for s in range(SLOTS):
            row = jnp.sum(jnp.where(rank == float(s), value, 0.0), axis=0, keepdims=True)
            slots.append(jnp.broadcast_to(row, (16, 128)))
        code = jnp.transpose(jnp.concatenate(slots, axis=0)).astype(I32) - 1
        code_v[l] = code
        low_v[l] = code & 127
        high_v[l] = lax.shift_right_arithmetic(code, 7)

    loads[1].wait()
    loads[2].wait()
    loads[3].wait()
    loads[4].start()
    xf[...] = x_v[...].astype(F32)
    own = jnp.where(r == 0, 1.0, 0.0)
    for l in range(LAYERS):
        x_l = xf[pl.ds(l, TOKENS, stride=4), :]
        dense[l] = (jnp.dot(x_l.astype(BF16), enc_v[l], preferred_element_type=F32)
                    + bias_v[pl.ds(l, 1), :] * own)

    def gather(l, carry):
        own_lane = (lax.broadcasted_iota(I32, (TOKENS, 128), 1) & 15) == (
            lax.broadcasted_iota(I32, (TOKENS, 128), 0) & 15)
        low = low_v[l]
        high = high_v[l]
        got = jnp.zeros((TOKENS, 128), F32)
        for h in range(8):
            block = dense[l, :, pl.ds(h * 128, 128)]
            got = jnp.where(high == h, pick(block, low), got)
        got = jnp.where(own_lane, got, 0.0)
        ybuf[y, pl.ds(pl.multiple_of(l * 8, 8), 8), :] = jnp.sum(
            got.reshape(8, 16, 128), axis=1)
        return carry

    def send(src, dst, s_sem, r_sem, peer):
        copy = pltpu.make_async_remote_copy(
            src_ref=src, dst_ref=dst, send_sem=s_sem, recv_sem=r_sem,
            device_id=peer, device_id_type=MESH)
        copy.start()
        return copy

    def arrive(buf, other, s_sem, r_sem, peer):
        pltpu.make_async_remote_copy(
            src_ref=buf.at[other], dst_ref=buf.at[other], send_sem=s_sem,
            recv_sem=r_sem, device_id=peer, device_id_type=MESH).wait_recv()

    def exchange(buf, me, n, peer, s_sem, r_sem, between=None):
        sends = [send(buf.at[me], buf.at[me], s_sem.at[i], r_sem.at[me], peer(i))
                 for i in range(n - 1, 0, -1)]
        if between is not None:
            between()
        for i in range(1, n):
            other = lax.rem(me + i, n)
            arrive(buf, other, s_sem.at[i], r_sem.at[other], peer(i))
        for copy in sends:
            copy.wait_send()

    def total(buf, n):
        acc = buf[0].astype(F32)
        for i in range(1, n):
            acc = acc + buf[i].astype(F32)
        return acc

    def source_of(k):
        return jnp.where(k <= g, k, k - g - 1)

    def gather_decoder(begin, end):

        def build(hot, b):
            tokens = pl.ds(pl.multiple_of(b * 16, 16), 16)
            for l in range(LAYERS):
                code = code_v[l, tokens, :]
                for s in range(SLOTS):
                    at = jnp.broadcast_to(code[:, s * 16:s * 16 + 1], (16, 128))
                    for h in range(8):
                        hot[l, pl.ds(s * 16, 16), pl.ds(h * 128, 128)] = jnp.where(
                            at == lane16 + h * 128, 1.0, 0.0).astype(BF16)

        def multiply(hot, b):
            for k in range(BLOCKS):
                rows_v[b, pl.ds(k * 128, 128), :] = jnp.dot(
                    hot[source_of(k)], dec_v[k], preferred_element_type=F32).astype(BF16)

        def step(n, carry):
            build(hot_b, 2 * n + 1)
            multiply(hot_a, 2 * n)
            build(hot_a, jnp.minimum(2 * n + 2, 7))
            multiply(hot_b, 2 * n + 1)
            return carry

        if begin == 0:
            loads[4].wait()
            build(hot_a, 0)
        lax.fori_loop(begin, end, step, 0)

    def build_inverse():
        def step(b, carry):
            tokens = pl.ds(pl.multiple_of(b * 16, 16), 16)
            for l in range(LAYERS):
                code = code_v[l, tokens, :]
                found = [jnp.full((16, 128), -1, I32) for h in range(8)]
                for s in range(SLOTS):
                    at = jnp.broadcast_to(code[:, s * 16:s * 16 + 1], (16, 128))
                    for h in range(8):
                        found[h] = jnp.where(at == lane16 + h * 128, row16 + s * 16, found[h])
                for h in range(8):
                    inv[l, tokens, pl.ds(h * 128, 128)] = found[h]
            return carry

        lax.fori_loop(0, 8, step, 0)

    def prepare():
        gather_decoder(2, 4)
        for l in range(LAYERS):
            xt_ref[l] = jnp.transpose(xf[pl.ds(l, TOKENS, stride=4), :]).astype(BF16)
        loads[5].wait()
        loads[6].wait()
        goal_all = tgt_v[...].astype(F32)
        for c in range(2):
            goal[c] = goal_all[:, c, :]

    lax.fori_loop(0, LAYERS, gather, 0)
    pl.semaphore_wait(barrier, 23)
    exchange(ybuf, y, 4, ypeer, y_s, y_r, between=lambda: gather_decoder(0, 2))
    zbuf[zl] = total(ybuf, 4)
    exchange(zbuf, zl, 4, zpeer, z_s, z_r, between=prepare)
    val_v[...] = total(zbuf, 4).astype(BF16).astype(F32)

    def rebuild(b):
        zero = jnp.zeros((16, 128), F32)
        top, bottom = [], []
        for k in range(BLOCKS):
            row = val_v[pl.ds(source_of(k) * 8 + b, 1), :]
            block = jnp.where(mine, jnp.broadcast_to(row, (16, 128)), 0.0)
            if k == 0:
                top.append(block)
                bottom.append(zero)
            elif k == 1:
                top.append(block * jnp.where(g == 1, 1.0, 0.0))
                bottom.append(block * jnp.where(g == 1, 0.0, 1.0))
            else:
                top.append(zero)
                bottom.append(block)
        left = jnp.concatenate([jnp.concatenate(top, axis=1), jnp.concatenate(bottom, axis=1)],
                               axis=0)
        return jnp.dot(left.astype(BF16), rows_v[b],
                       preferred_element_type=F32).reshape(2, 16, FEAT)

    def give(i):
        other = lax.rem(q + i, 8)
        return send(rs_src.at[other], rs_buf.at[q], rs_s.at[i], rs_r.at[q], qpeer(i))

    order = (4, 3, 5, 2, 6, 1, 7)
    sends = []
    for n, i in enumerate(order):
        b = lax.rem(q + i, 8)
        rs_src[b] = rebuild(b).astype(BF16)
        if n > 0:
            sends.append(give(order[n - 1]))
    rs_buf[q] = rebuild(q).astype(BF16)
    sends.append(give(order[-1]))
    build_inverse()
    for i in range(1, 8):
        other = lax.rem(q + i, 8)
        arrive(rs_buf, other, rs_s.at[i], rs_r.at[other], qpeer(i))
    hbuf[zh] = total(rs_buf, 8).astype(BF16)
    copy = send(hbuf.at[zh], hbuf.at[zh], h_s, h_r.at[zh], hpeer)
    def spread(b, carry):
        for l in range(LAYERS):
            scatter(act_ref, val_v, inv, l, b)
        return carry

    lax.fori_loop(0, 8, spread, 0)
    for other in sends:
        other.wait_send()
    arrive(hbuf, 1 - zh, h_s, h_r.at[1 - zh], hpeer)
    copy.wait_send()
    rebuilt = total(hbuf, 2)
    for c in range(2):
        abuf[q, c] = (rebuilt[c] + dbias_v[pl.ds(c, 1), :] - goal[c]).astype(BF16)

    def back(b):
        out = lax.dot_general(abuf[b].reshape(32, FEAT), rows_v[b], (((1,), (1,)), ((), ())),
                              preferred_element_type=F32)

        def part(c, k):
            block = out[c * 16:c * 16 + 16, k * 128:k * 128 + 128]
            return jnp.sum(jnp.where(mine, block, 0.0), axis=0, keepdims=True)

        p0 = part(0, 0)
        p1 = jnp.where(g == 1, part(0, 1), part(1, 1))
        p2, p3, p4 = part(1, 2), part(1, 3), part(1, 4)
        pay_v[pl.ds(b, 1), :] = p0 + jnp.where(g == 1, p2, p1)
        pay_v[pl.ds(8 + b, 1), :] = jnp.where(g == 1, p1 + p3, p2)
        pay_v[pl.ds(16 + b, 1), :] = jnp.where(g == 1, p4, p3)
        pay_v[pl.ds(24 + b, 1), :] = jnp.where(g == 1, jnp.zeros_like(p4), p4)

    sends = [send(abuf.at[q], abuf.at[q], ag_s.at[i], ag_r.at[q], qpeer(i)) for i in order]
    back(q)
    for i in (1, 7, 2, 6, 3, 5, 4):
        other = lax.rem(q + i, 8)
        arrive(abuf, other, ag_s.at[i], ag_r.at[other], qpeer(i))
        back(other)
    for copy in sends:
        copy.wait_send()
    lbuf[r] = pay_v[...].astype(BF16)

    def keep_residue():
        res_ref[...] = abuf[...]

    exchange(lbuf, r, 16, lpeer, l_s, l_r, between=keep_residue)
    pick_ref[...] = total(lbuf, 16).astype(BF16).astype(F32)


def main_call(x, enc, bias, dec, dbias, tgt, idx):
    dma = pltpu.SemaphoreType.DMA
    vmem = pltpu.VMEM
    return pl.pallas_call(
        main_kernel,
        out_shape=(
            jax.ShapeDtypeStruct((LAYERS, TOKENS, WIDTH), BF16),
            jax.ShapeDtypeStruct((8, 2, 16, FEAT), BF16),
            jax.ShapeDtypeStruct((32, 128), F32),
            jax.ShapeDtypeStruct((LAYERS, TOKENS, WIDTH), I32),
            jax.ShapeDtypeStruct((LAYERS, DIN, TOKENS), BF16),
        ),
        in_specs=[pl.BlockSpec(memory_space=pltpu.HBM)] * 7,
        out_specs=(pl.BlockSpec(memory_space=pltpu.VMEM),) * 5,
        scratch_shapes=[
            vmem((TOKENS * LAYERS, DIN), BF16),
            vmem((LAYERS, DIN, WIDTH), BF16),
            vmem((LAYERS, WIDTH), F32),
            vmem((BLOCKS, WIDTH, FEAT), BF16),
            vmem((2, FEAT), F32),
            vmem((16, 2, FEAT), BF16),
            vmem((LAYERS, TOPK, TOKENS), I32),
            dma((7,)),
            vmem((TOKENS * LAYERS, DIN), F32),
            vmem((LAYERS, TOKENS, WIDTH), F32),
            vmem((LAYERS, TOKENS, 128), I32),
            vmem((LAYERS, TOKENS, 128), I32),
            vmem((LAYERS, TOKENS, 128), I32),
            vmem((LAYERS, 128, WIDTH), BF16),
            vmem((LAYERS, 128, WIDTH), BF16),
            vmem((8, BLOCKS * 128, FEAT), BF16),
            vmem((32, 128), F32),
            vmem((32, 128), F32),
            vmem((2, 16, FEAT), F32),
            vmem((4, 32, 128), F32),
            vmem((4, 32, 128), F32),
            vmem((16, 32, 128), BF16),
            vmem((8, 2, 16, FEAT), BF16),
            vmem((8, 2, 16, FEAT), BF16),
            vmem((2, 2, 16, FEAT), BF16),
            vmem((8, 2, 16, FEAT), BF16),
            dma((4,)), dma((4,)), dma((4,)), dma((4,)), dma((16,)), dma((16,)),
            dma((8,)), dma((8,)), dma, dma((2,)), dma((8,)), dma((8,)),
        ],
        compiler_params=pltpu.CompilerParams(collective_id=0, has_side_effects=True,
                                             vmem_limit_bytes=28 * 2**20),
        name="transcoder",
    )(*[pltpu.with_memory_space_constraint(v, pltpu.HBM)
        for v in (x, enc, bias, dec, dbias, tgt, idx)])


def grad_kernel(act_ref, res_ref, pick_ref, inv_ref, xt_ref, dg_hbm, eg_hbm, bg_ref,
                dg_v, eg_v, pg_v, sem):
    g = lax.div(lax.axis_index("layer"), 8)
    copies = []
    for k in range(BLOCKS):
        source = jnp.where(k <= g, k, k - g - 1)
        slot = jnp.where(k <= g, 0, 1)
        residue = res_ref[:, slot].reshape(TOKENS, FEAT)
        dg_v[k] = lax.dot_general(act_ref[source], residue, (((0,), (0,)), ((), ())),
                                  preferred_element_type=F32)
        copies.append(pltpu.make_async_copy(dg_v.at[k], dg_hbm.at[k], sem.at[k]))
        copies[-1].start()
    def layer(l, carry):
        for b in range(8):
            scatter(pg_v, pick_ref, inv_ref, l, b)
        grads = pg_v[l]
        eg_v[l] = jnp.dot(xt_ref[l], grads, preferred_element_type=F32)
        pltpu.make_async_copy(eg_v.at[l], eg_hbm.at[l], sem.at[BLOCKS + l]).start()
        bg_ref[pl.ds(l, 1), :] = jnp.dot(jnp.ones((8, TOKENS), BF16), grads,
                                         preferred_element_type=F32)[0:1]
        return carry

    lax.fori_loop(0, LAYERS, layer, 0)
    for l in range(LAYERS):
        pltpu.make_async_copy(eg_v.at[l], eg_hbm.at[l], sem.at[BLOCKS + l]).wait()
    for copy in copies:
        copy.wait()


def grad_call(act, res, picked, inv, xt):
    vmem = pltpu.VMEM
    return pl.pallas_call(
        grad_kernel,
        out_shape=(
            jax.ShapeDtypeStruct((BLOCKS, WIDTH, FEAT), F32),
            jax.ShapeDtypeStruct((LAYERS, DIN, WIDTH), F32),
            jax.ShapeDtypeStruct((LAYERS, WIDTH), F32),
        ),
        in_specs=[pl.BlockSpec(memory_space=vmem)] * 5,
        out_specs=(pl.BlockSpec(memory_space=pl.ANY), pl.BlockSpec(memory_space=pl.ANY),
                   pl.BlockSpec(memory_space=vmem)),
        scratch_shapes=[vmem((BLOCKS, WIDTH, FEAT), F32), vmem((LAYERS, DIN, WIDTH), F32),
                        vmem((LAYERS, TOKENS, WIDTH), BF16),
                        pltpu.SemaphoreType.DMA((BLOCKS + LAYERS,))],
        compiler_params=pltpu.CompilerParams(vmem_limit_bytes=24 * 2**20),
        name="weight_grads",
    )(act, res, picked, inv, xt)


def body(inputs, encoder, enc_bias, decoder, dec_bias, targets, top_index):
    act, res, picked, inv, xt = main_call(
        inputs.reshape(TOKENS * LAYERS, DIN), encoder, enc_bias, decoder[0], dec_bias[0],
        targets[0], jnp.transpose(top_index, (1, 2, 0)))
    dg, eg, bg = grad_call(act, res, picked, inv, xt)
    return dg[None], eg, bg


def solution(mesh):
    return jax.shard_map(
        body,
        mesh=mesh,
        in_specs=(
            P(None, None, "layer"),
            P(None, "layer", "lat"),
            P(None, "lat"),
            P("layer", None, "lat", None),
            P("layer", None, None),
            P("layer", None, None, None),
            P(),
        ),
        out_specs=(P("layer", None, "lat", None), P(None, "layer", "lat"), P(None, "lat")),
        check_vma=False,
    )
```

```python
import jax
import jax.numpy as jnp
from jax import lax
from jax.experimental import pallas as pl
from jax.experimental.pallas import tpu as pltpu
from jax.sharding import PartitionSpec as P

MESH = pl.DeviceIdType.MESH
F32 = jnp.float32
BF16 = jnp.bfloat16
I32 = jnp.int32

TOKENS, LAYERS, TOPK, WIDTH, DIN, FEAT, BLOCKS, SLOTS = 128, 4, 64, 1024, 128, 256, 5, 8


def pick(values, lanes):
    return jnp.take_along_axis(values, lanes, axis=1, mode="promise_in_bounds")


def scatter(out_ref, values_ref, inv_ref, l, b):
    rows = pl.ds(pl.multiple_of(b * 16, 16), 16)
    values = jnp.broadcast_to(values_ref[pl.ds(l * 8 + b, 1), :], (16, 128))
    for h in range(8):
        cols = pl.ds(h * 128, 128)
        where = inv_ref[l, rows, cols]
        got = jnp.where(where >= 0, pick(values, where & 127), 0.0)
        out_ref[l, rows, cols] = got.astype(BF16)


def main_kernel(x_hbm, enc_hbm, bias_hbm, dec_hbm, dbias_hbm, tgt_hbm, idx_hbm,
                dg_ref, pick_ref, inv, xt_ref,
                x_v, enc_v, bias_v, dec_v, dbias_v, tgt_v, idx_v, load_sem,
                xf, dense, code_v, low_v, high_v, hot_a, hot_b, rows_v, val_v, pay_v, goal,
                act_v, ybuf, zbuf, lbuf, rs_src, rs_buf, hbuf, abuf,
                y_s, y_r, z_s, z_r, l_s, l_r, rs_s, rs_r, h_s, h_r, ag_s, ag_r):
    r = lax.axis_index("layer")
    j = lax.axis_index("lat")
    y = lax.rem(r, 4)
    zl = lax.div(r, 4)
    q = lax.rem(j, 8)
    zh = lax.div(j, 8)
    g = lax.div(r, 8)

    loads = [
        pltpu.make_async_copy(idx_hbm, idx_v, load_sem.at[0]),
        pltpu.make_async_copy(x_hbm, x_v, load_sem.at[1]),
        pltpu.make_async_copy(enc_hbm, enc_v, load_sem.at[2]),
        pltpu.make_async_copy(bias_hbm, bias_v, load_sem.at[3]),
        pltpu.make_async_copy(dec_hbm, dec_v, load_sem.at[4]),
        pltpu.make_async_copy(dbias_hbm, dbias_v, load_sem.at[5]),
        pltpu.make_async_copy(tgt_hbm.at[pl.ds(q * 16, 16)], tgt_v, load_sem.at[6]),
    ]
    for n in (0, 1, 2, 3, 5, 6):
        loads[n].start()

    def ypeer(i):
        return {"layer": zl * 4 + lax.rem(y + i, 4)}

    def zpeer(i):
        return {"layer": lax.rem(zl + i, 4) * 4 + y}

    def lpeer(i):
        return {"layer": lax.rem(r + i, 16)}

    def qpeer(i):
        return {"lat": zh * 8 + lax.rem(q + i, 8)}

    hpeer = {"lat": (1 - zh) * 8 + q}

    barrier = pltpu.get_barrier_semaphore()
    for i in range(1, 16):
        pl.semaphore_signal(barrier, inc=1, device_id=lpeer(i), device_id_type=MESH)
    for i in range(1, 8):
        pl.semaphore_signal(barrier, inc=1, device_id=qpeer(i), device_id_type=MESH)
    pl.semaphore_signal(barrier, inc=1, device_id=hpeer, device_id_type=MESH)

    lane16 = lax.broadcasted_iota(I32, (16, 128), 1)
    row16 = lax.broadcasted_iota(I32, (16, 128), 0)
    mine = (lane16 & 15) == row16

    loads[0].wait()
    tri = (lax.broadcasted_iota(I32, (TOPK, TOPK), 1)
           < lax.broadcasted_iota(I32, (TOPK, TOPK), 0)).astype(F32).astype(BF16)
    for l in range(LAYERS):
        local = idx_v[l] - j * WIDTH
        inside = (local >= 0) & (local < WIDTH)
        rank = jnp.dot(tri, inside.astype(F32).astype(BF16), preferred_element_type=F32)
        rank = jnp.where(inside, rank, -1.0)
        value = (local + 1).astype(F32)
        slots = []
        for s in range(SLOTS):
            row = jnp.sum(jnp.where(rank == float(s), value, 0.0), axis=0, keepdims=True)
            slots.append(jnp.broadcast_to(row, (16, 128)))
        code = jnp.transpose(jnp.concatenate(slots, axis=0)).astype(I32) - 1
        code_v[l] = code
        low_v[l] = code & 127
        high_v[l] = lax.shift_right_arithmetic(code, 7)

    loads[1].wait()
    loads[2].wait()
    loads[3].wait()
    loads[4].start()
    xf[...] = x_v[...].astype(F32)
    own = jnp.where(r == 0, 1.0, 0.0)
    for l in range(LAYERS):
        x_l = xf[pl.ds(l, TOKENS, stride=4), :]
        dense[l] = (jnp.dot(x_l.astype(BF16), enc_v[l], preferred_element_type=F32)
                    + bias_v[pl.ds(l, 1), :] * own)

    def gather(l, carry):
        own_lane = (lax.broadcasted_iota(I32, (TOKENS, 128), 1) & 15) == (
            lax.broadcasted_iota(I32, (TOKENS, 128), 0) & 15)
        low = low_v[l]
        high = high_v[l]
        got = jnp.zeros((TOKENS, 128), F32)
        for h in range(8):
            block = dense[l, :, pl.ds(h * 128, 128)]
            got = jnp.where(high == h, pick(block, low), got)
        got = jnp.where(own_lane, got, 0.0)
        ybuf[y, pl.ds(pl.multiple_of(l * 8, 8), 8), :] = jnp.sum(
            got.reshape(8, 16, 128), axis=1)
        return carry

    def send(src, dst, s_sem, r_sem, peer):
        copy = pltpu.make_async_remote_copy(
            src_ref=src, dst_ref=dst, send_sem=s_sem, recv_sem=r_sem,
            device_id=peer, device_id_type=MESH)
        copy.start()
        return copy

    def arrive(buf, other, s_sem, r_sem, peer):
        pltpu.make_async_remote_copy(
            src_ref=buf.at[other], dst_ref=buf.at[other], send_sem=s_sem,
            recv_sem=r_sem, device_id=peer, device_id_type=MESH).wait_recv()

    def exchange(buf, me, n, peer, s_sem, r_sem, between=None):
        sends = [send(buf.at[me], buf.at[me], s_sem.at[i], r_sem.at[me], peer(i))
                 for i in range(n - 1, 0, -1)]
        if between is not None:
            between()
        for i in range(1, n):
            other = lax.rem(me + i, n)
            arrive(buf, other, s_sem.at[i], r_sem.at[other], peer(i))
        for copy in sends:
            copy.wait_send()

    def total(buf, n):
        acc = buf[0].astype(F32)
        for i in range(1, n):
            acc = acc + buf[i].astype(F32)
        return acc

    def source_of(k):
        return jnp.where(k <= g, k, k - g - 1)

    def gather_decoder(begin, end):

        def build(hot, b):
            tokens = pl.ds(pl.multiple_of(b * 16, 16), 16)
            for l in range(LAYERS):
                code = code_v[l, tokens, :]
                for s in range(SLOTS):
                    at = jnp.broadcast_to(code[:, s * 16:s * 16 + 1], (16, 128))
                    for h in range(8):
                        hot[l, pl.ds(s * 16, 16), pl.ds(h * 128, 128)] = jnp.where(
                            at == lane16 + h * 128, 1.0, 0.0).astype(BF16)

        def multiply(hot, b):
            for k in range(BLOCKS):
                rows_v[b, pl.ds(k * 128, 128), :] = jnp.dot(
                    hot[source_of(k)], dec_v[k], preferred_element_type=F32).astype(BF16)

        def step(n, carry):
            build(hot_b, 2 * n + 1)
            multiply(hot_a, 2 * n)
            build(hot_a, jnp.minimum(2 * n + 2, 7))
            multiply(hot_b, 2 * n + 1)
            return carry

        if begin == 0:
            loads[4].wait()
            build(hot_a, 0)
        lax.fori_loop(begin, end, step, 0)

    def build_inverse():
        def step(b, carry):
            tokens = pl.ds(pl.multiple_of(b * 16, 16), 16)
            for l in range(LAYERS):
                code = code_v[l, tokens, :]
                found = [jnp.full((16, 128), -1, I32) for h in range(8)]
                for s in range(SLOTS):
                    at = jnp.broadcast_to(code[:, s * 16:s * 16 + 1], (16, 128))
                    for h in range(8):
                        found[h] = jnp.where(at == lane16 + h * 128, row16 + s * 16, found[h])
                for h in range(8):
                    inv[l, tokens, pl.ds(h * 128, 128)] = found[h]
            return carry

        lax.fori_loop(0, 8, step, 0)

    def prepare():
        gather_decoder(2, 4)
        for l in range(LAYERS):
            xt_ref[l] = jnp.transpose(xf[pl.ds(l, TOKENS, stride=4), :]).astype(BF16)
        loads[5].wait()
        loads[6].wait()
        goal_all = tgt_v[...].astype(F32)
        for c in range(2):
            goal[c] = goal_all[:, c, :]

    lax.fori_loop(0, LAYERS, gather, 0)
    pl.semaphore_wait(barrier, 23)
    exchange(ybuf, y, 4, ypeer, y_s, y_r, between=lambda: gather_decoder(0, 2))
    zbuf[zl] = total(ybuf, 4)
    exchange(zbuf, zl, 4, zpeer, z_s, z_r, between=prepare)
    val_v[...] = total(zbuf, 4).astype(BF16).astype(F32)

    def rebuild(b):
        zero = jnp.zeros((16, 128), F32)
        top, bottom = [], []
        for k in range(BLOCKS):
            row = val_v[pl.ds(source_of(k) * 8 + b, 1), :]
            block = jnp.where(mine, jnp.broadcast_to(row, (16, 128)), 0.0)
            if k == 0:
                top.append(block)
                bottom.append(zero)
            elif k == 1:
                top.append(block * jnp.where(g == 1, 1.0, 0.0))
                bottom.append(block * jnp.where(g == 1, 0.0, 1.0))
            else:
                top.append(zero)
                bottom.append(block)
        left = jnp.concatenate([jnp.concatenate(top, axis=1), jnp.concatenate(bottom, axis=1)],
                               axis=0)
        return jnp.dot(left.astype(BF16), rows_v[b],
                       preferred_element_type=F32).reshape(2, 16, FEAT)

    def give(i):
        other = lax.rem(q + i, 8)
        return send(rs_src.at[other], rs_buf.at[q], rs_s.at[i], rs_r.at[q], qpeer(i))

    order = (4, 3, 5, 2, 6, 1, 7)
    sends = []
    for n, i in enumerate(order):
        b = lax.rem(q + i, 8)
        rs_src[b] = rebuild(b).astype(BF16)
        if n > 0:
            sends.append(give(order[n - 1]))
    rs_buf[q] = rebuild(q).astype(BF16)
    sends.append(give(order[-1]))
    build_inverse()
    for i in range(1, 8):
        other = lax.rem(q + i, 8)
        arrive(rs_buf, other, rs_s.at[i], rs_r.at[other], qpeer(i))
    hbuf[zh] = total(rs_buf, 8).astype(BF16)
    copy = send(hbuf.at[zh], hbuf.at[zh], h_s, h_r.at[zh], hpeer)
    def spread(b, carry):
        for l in range(LAYERS):
            scatter(act_v, val_v, inv, l, b)
        return carry

    lax.fori_loop(0, 8, spread, 0)
    for other in sends:
        other.wait_send()
    arrive(hbuf, 1 - zh, h_s, h_r.at[1 - zh], hpeer)
    copy.wait_send()
    rebuilt = total(hbuf, 2)
    for c in range(2):
        abuf[q, c] = (rebuilt[c] + dbias_v[pl.ds(c, 1), :] - goal[c]).astype(BF16)

    def back(b):
        out = lax.dot_general(abuf[b].reshape(32, FEAT), rows_v[b], (((1,), (1,)), ((), ())),
                              preferred_element_type=F32)

        def part(c, k):
            block = out[c * 16:c * 16 + 16, k * 128:k * 128 + 128]
            return jnp.sum(jnp.where(mine, block, 0.0), axis=0, keepdims=True)

        p0 = part(0, 0)
        p1 = jnp.where(g == 1, part(0, 1), part(1, 1))
        p2, p3, p4 = part(1, 2), part(1, 3), part(1, 4)
        pay_v[pl.ds(b, 1), :] = p0 + jnp.where(g == 1, p2, p1)
        pay_v[pl.ds(8 + b, 1), :] = jnp.where(g == 1, p1 + p3, p2)
        pay_v[pl.ds(16 + b, 1), :] = jnp.where(g == 1, p4, p3)
        pay_v[pl.ds(24 + b, 1), :] = jnp.where(g == 1, jnp.zeros_like(p4), p4)

    sends = [send(abuf.at[q], abuf.at[q], ag_s.at[i], ag_r.at[q], qpeer(i)) for i in order]
    back(q)
    for i in (1, 7, 2, 6, 3, 5, 4):
        other = lax.rem(q + i, 8)
        arrive(abuf, other, ag_s.at[i], ag_r.at[other], qpeer(i))
        back(other)
    for copy in sends:
        copy.wait_send()
    lbuf[r] = pay_v[...].astype(BF16)

    def decoder_grads():
        for k in range(BLOCKS):
            residue = abuf[:, jnp.where(k <= g, 0, 1)].reshape(TOKENS, FEAT)
            dg_ref[k] = lax.dot_general(act_v[source_of(k)], residue, (((0,), (0,)), ((), ())),
                                        preferred_element_type=F32)

    exchange(lbuf, r, 16, lpeer, l_s, l_r, between=decoder_grads)
    pick_ref[...] = total(lbuf, 16).astype(BF16).astype(F32)


def main_call(x, enc, bias, dec, dbias, tgt, idx):
    dma = pltpu.SemaphoreType.DMA
    vmem = pltpu.VMEM
    return pl.pallas_call(
        main_kernel,
        out_shape=(
            jax.ShapeDtypeStruct((BLOCKS, WIDTH, FEAT), F32),
            jax.ShapeDtypeStruct((32, 128), F32),
            jax.ShapeDtypeStruct((LAYERS, TOKENS, WIDTH), I32),
            jax.ShapeDtypeStruct((LAYERS, DIN, TOKENS), BF16),
        ),
        in_specs=[pl.BlockSpec(memory_space=pltpu.HBM)] * 7,
        out_specs=(pl.BlockSpec(memory_space=pltpu.VMEM),) * 4,
        scratch_shapes=[
            vmem((TOKENS * LAYERS, DIN), BF16),
            vmem((LAYERS, DIN, WIDTH), BF16),
            vmem((LAYERS, WIDTH), F32),
            vmem((BLOCKS, WIDTH, FEAT), BF16),
            vmem((2, FEAT), F32),
            vmem((16, 2, FEAT), BF16),
            vmem((LAYERS, TOPK, TOKENS), I32),
            dma((7,)),
            vmem((TOKENS * LAYERS, DIN), F32),
            vmem((LAYERS, TOKENS, WIDTH), F32),
            vmem((LAYERS, TOKENS, 128), I32),
            vmem((LAYERS, TOKENS, 128), I32),
            vmem((LAYERS, TOKENS, 128), I32),
            vmem((LAYERS, 128, WIDTH), BF16),
            vmem((LAYERS, 128, WIDTH), BF16),
            vmem((8, BLOCKS * 128, FEAT), BF16),
            vmem((32, 128), F32),
            vmem((32, 128), F32),
            vmem((2, 16, FEAT), F32),
            vmem((LAYERS, TOKENS, WIDTH), BF16),
            vmem((4, 32, 128), F32),
            vmem((4, 32, 128), F32),
            vmem((16, 32, 128), BF16),
            vmem((8, 2, 16, FEAT), BF16),
            vmem((8, 2, 16, FEAT), BF16),
            vmem((2, 2, 16, FEAT), BF16),
            vmem((8, 2, 16, FEAT), BF16),
            dma((4,)), dma((4,)), dma((4,)), dma((4,)), dma((16,)), dma((16,)),
            dma((8,)), dma((8,)), dma, dma((2,)), dma((8,)), dma((8,)),
        ],
        compiler_params=pltpu.CompilerParams(collective_id=0, has_side_effects=True,
                                             vmem_limit_bytes=28 * 2**20),
        name="transcoder",
    )(*[pltpu.with_memory_space_constraint(v, pltpu.HBM)
        for v in (x, enc, bias, dec, dbias, tgt, idx)])


def grad_kernel(dg_ref, pick_ref, inv_ref, xt_ref, dg_hbm, eg_hbm, bg_ref, eg_v, pg_v, sem):
    copies = [pltpu.make_async_copy(dg_ref.at[k], dg_hbm.at[k], sem.at[k])
              for k in range(BLOCKS)]
    for copy in copies:
        copy.start()

    def layer(l, carry):
        for b in range(8):
            scatter(pg_v, pick_ref, inv_ref, l, b)
        grads = pg_v[l]
        eg_v[l] = jnp.dot(xt_ref[l], grads, preferred_element_type=F32)
        pltpu.make_async_copy(eg_v.at[l], eg_hbm.at[l], sem.at[BLOCKS + l]).start()
        bg_ref[pl.ds(l, 1), :] = jnp.dot(jnp.ones((8, TOKENS), BF16), grads,
                                         preferred_element_type=F32)[0:1]
        return carry

    lax.fori_loop(0, LAYERS, layer, 0)
    for l in range(LAYERS):
        pltpu.make_async_copy(eg_v.at[l], eg_hbm.at[l], sem.at[BLOCKS + l]).wait()
    for copy in copies:
        copy.wait()


def grad_call(dg, picked, inv, xt):
    vmem = pltpu.VMEM
    return pl.pallas_call(
        grad_kernel,
        out_shape=(
            jax.ShapeDtypeStruct((BLOCKS, WIDTH, FEAT), F32),
            jax.ShapeDtypeStruct((LAYERS, DIN, WIDTH), F32),
            jax.ShapeDtypeStruct((LAYERS, WIDTH), F32),
        ),
        in_specs=[pl.BlockSpec(memory_space=vmem)] * 4,
        out_specs=(pl.BlockSpec(memory_space=pl.ANY), pl.BlockSpec(memory_space=pl.ANY),
                   pl.BlockSpec(memory_space=vmem)),
        scratch_shapes=[vmem((LAYERS, DIN, WIDTH), F32),
                        vmem((LAYERS, TOKENS, WIDTH), BF16),
                        pltpu.SemaphoreType.DMA((BLOCKS + LAYERS,))],
        compiler_params=pltpu.CompilerParams(vmem_limit_bytes=24 * 2**20),
        name="weight_grads",
    )(dg, picked, inv, xt)


def body(inputs, encoder, enc_bias, decoder, dec_bias, targets, top_index):
    dg, picked, inv, xt = main_call(
        inputs.reshape(TOKENS * LAYERS, DIN), encoder, enc_bias, decoder[0], dec_bias[0],
        targets[0], jnp.transpose(top_index, (1, 2, 0)))
    dg, eg, bg = grad_call(dg, picked, inv, xt)
    return dg[None], eg, bg


def solution(mesh):
    return jax.shard_map(
        body,
        mesh=mesh,
        in_specs=(
            P(None, None, "layer"),
            P(None, "layer", "lat"),
            P(None, "lat"),
            P("layer", None, "lat", None),
            P("layer", None, None),
            P("layer", None, None, None),
            P(),
        ),
        out_specs=(P("layer", None, "lat", None), P(None, "layer", "lat"), P(None, "lat")),
        check_vma=False,
    )
```

```python
import jax
import jax.numpy as jnp
from jax import lax
from jax.experimental import pallas as pl
from jax.experimental.pallas import tpu as pltpu
from jax.sharding import PartitionSpec as P

MESH = pl.DeviceIdType.MESH
F32 = jnp.float32
BF16 = jnp.bfloat16
I32 = jnp.int32

TOKENS, LAYERS, TOPK, WIDTH, DIN, FEAT, BLOCKS, SLOTS = 128, 4, 64, 1024, 128, 256, 5, 8


def pick(values, lanes):
    return jnp.take_along_axis(values, lanes, axis=1, mode="promise_in_bounds")


def scatter(out_ref, values_ref, inv_ref, l, b):
    rows = pl.ds(pl.multiple_of(b * 16, 16), 16)
    values = jnp.broadcast_to(values_ref[pl.ds(l * 8 + b, 1), :], (16, 128))
    for h in range(8):
        cols = pl.ds(h * 128, 128)
        where = inv_ref[l, rows, cols]
        got = jnp.where(where >= 0, pick(values, where & 127), 0.0)
        out_ref[l, rows, cols] = got.astype(BF16)


def main_kernel(x_hbm, enc_hbm, bias_hbm, dec_hbm, dbias_hbm, tgt_hbm, idx_hbm,
                dg_ref, pick_ref, inv, xt_ref,
                x_v, enc_v, bias_v, dec_v, dbias_v, tgt_v, idx_v, load_sem,
                xf, dense, code_v, low_v, high_v, hot_a, hot_b, rows_v, val_v, pay_v, goal,
                act_v, ybuf, zbuf, lbuf, rs_src, rs_buf, hbuf, abuf,
                y_s, y_r, z_s, z_r, l_s, l_r, rs_s, rs_r, h_s, h_r, ag_s, ag_r):
    r = lax.axis_index("layer")
    j = lax.axis_index("lat")
    y = lax.rem(r, 4)
    zl = lax.div(r, 4)
    q = lax.rem(j, 8)
    zh = lax.div(j, 8)
    g = lax.div(r, 8)

    loads = [
        pltpu.make_async_copy(idx_hbm, idx_v, load_sem.at[0]),
        pltpu.make_async_copy(x_hbm, x_v, load_sem.at[1]),
        pltpu.make_async_copy(enc_hbm, enc_v, load_sem.at[2]),
        pltpu.make_async_copy(bias_hbm, bias_v, load_sem.at[3]),
        pltpu.make_async_copy(dec_hbm, dec_v, load_sem.at[4]),
        pltpu.make_async_copy(dbias_hbm, dbias_v, load_sem.at[5]),
        pltpu.make_async_copy(tgt_hbm.at[pl.ds(q * 16, 16)], tgt_v, load_sem.at[6]),
    ]
    for n in (0, 1, 2, 3, 5, 6):
        loads[n].start()

    def ypeer(i):
        return {"layer": zl * 4 + lax.rem(y + i, 4)}

    def zpeer(i):
        return {"layer": lax.rem(zl + i, 4) * 4 + y}

    def lpeer(i):
        return {"layer": lax.rem(r + i, 16)}

    def qpeer(i):
        return {"lat": zh * 8 + lax.rem(q + i, 8)}

    hpeer = {"lat": (1 - zh) * 8 + q}

    barrier = pltpu.get_barrier_semaphore()
    for i in range(1, 16):
        pl.semaphore_signal(barrier, inc=1, device_id=lpeer(i), device_id_type=MESH)
    for i in range(1, 8):
        pl.semaphore_signal(barrier, inc=1, device_id=qpeer(i), device_id_type=MESH)
    pl.semaphore_signal(barrier, inc=1, device_id=hpeer, device_id_type=MESH)

    lane16 = lax.broadcasted_iota(I32, (16, 128), 1)
    row16 = lax.broadcasted_iota(I32, (16, 128), 0)
    mine = (lane16 & 15) == row16

    loads[0].wait()
    tri = (lax.broadcasted_iota(I32, (TOPK, TOPK), 1)
           < lax.broadcasted_iota(I32, (TOPK, TOPK), 0)).astype(F32).astype(BF16)
    for l in range(LAYERS):
        local = idx_v[l] - j * WIDTH
        inside = (local >= 0) & (local < WIDTH)
        rank = jnp.dot(tri, inside.astype(F32).astype(BF16), preferred_element_type=F32)
        rank = jnp.where(inside, rank, -1.0)
        value = (local + 1).astype(F32)
        slots = []
        for s in range(SLOTS):
            row = jnp.sum(jnp.where(rank == float(s), value, 0.0), axis=0, keepdims=True)
            slots.append(jnp.broadcast_to(row, (16, 128)))
        code = jnp.transpose(jnp.concatenate(slots, axis=0)).astype(I32) - 1
        code_v[l] = code
        low_v[l] = code & 127
        high_v[l] = lax.shift_right_arithmetic(code, 7)

    loads[1].wait()
    loads[2].wait()
    loads[3].wait()
    loads[4].start()
    xf[...] = x_v[...].astype(F32)
    own = jnp.where(r == 0, 1.0, 0.0)
    for l in range(LAYERS):
        x_l = xf[pl.ds(l, TOKENS, stride=4), :]
        dense[l] = (jnp.dot(x_l.astype(BF16), enc_v[l], preferred_element_type=F32)
                    + bias_v[pl.ds(l, 1), :] * own)

    def gather(l, carry):
        own_lane = (lax.broadcasted_iota(I32, (TOKENS, 128), 1) & 15) == (
            lax.broadcasted_iota(I32, (TOKENS, 128), 0) & 15)
        low = low_v[l]
        high = high_v[l]
        got = jnp.zeros((TOKENS, 128), F32)
        for h in range(8):
            block = dense[l, :, pl.ds(h * 128, 128)]
            got = jnp.where(high == h, pick(block, low), got)
        got = jnp.where(own_lane, got, 0.0)
        ybuf[y, pl.ds(pl.multiple_of(l * 8, 8), 8), :] = jnp.sum(
            got.reshape(8, 16, 128), axis=1)
        return carry

    def send(src, dst, s_sem, r_sem, peer):
        copy = pltpu.make_async_remote_copy(
            src_ref=src, dst_ref=dst, send_sem=s_sem, recv_sem=r_sem,
            device_id=peer, device_id_type=MESH)
        copy.start()
        return copy

    def arrive(buf, other, s_sem, r_sem, peer):
        pltpu.make_async_remote_copy(
            src_ref=buf.at[other], dst_ref=buf.at[other], send_sem=s_sem,
            recv_sem=r_sem, device_id=peer, device_id_type=MESH).wait_recv()

    pending = []

    def exchange(buf, me, n, peer, s_sem, r_sem, between=None):
        sends = [send(buf.at[me], buf.at[me], s_sem.at[i], r_sem.at[me], peer(i))
                 for i in range(n - 1, 0, -1)]
        if between is not None:
            between()
        for i in range(1, n):
            other = lax.rem(me + i, n)
            arrive(buf, other, s_sem.at[i], r_sem.at[other], peer(i))
        pending.extend(sends)

    def total(buf, n):
        acc = buf[0].astype(F32)
        for i in range(1, n):
            acc = acc + buf[i].astype(F32)
        return acc

    def source_of(k):
        return jnp.where(k <= g, k, k - g - 1)

    def gather_decoder(begin, end):

        def build(hot, b):
            tokens = pl.ds(pl.multiple_of(b * 16, 16), 16)
            for l in range(LAYERS):
                code = code_v[l, tokens, :]
                for s in range(SLOTS):
                    at = jnp.broadcast_to(code[:, s * 16:s * 16 + 1], (16, 128))
                    for h in range(8):
                        hot[l, pl.ds(s * 16, 16), pl.ds(h * 128, 128)] = jnp.where(
                            at == lane16 + h * 128, 1.0, 0.0).astype(BF16)

        def multiply(hot, b):
            for k in range(BLOCKS):
                rows_v[b, pl.ds(k * 128, 128), :] = jnp.dot(
                    hot[source_of(k)], dec_v[k], preferred_element_type=F32).astype(BF16)

        def step(n, carry):
            build(hot_b, 2 * n + 1)
            multiply(hot_a, 2 * n)
            build(hot_a, jnp.minimum(2 * n + 2, 7))
            multiply(hot_b, 2 * n + 1)
            return carry

        if begin == 0:
            loads[4].wait()
            build(hot_a, 0)
        lax.fori_loop(begin, end, step, 0)

    def build_inverse():
        def step(b, carry):
            tokens = pl.ds(pl.multiple_of(b * 16, 16), 16)
            for l in range(LAYERS):
                code = code_v[l, tokens, :]
                found = [jnp.full((16, 128), -1, I32) for h in range(8)]
                for s in range(SLOTS):
                    at = jnp.broadcast_to(code[:, s * 16:s * 16 + 1], (16, 128))
                    for h in range(8):
                        found[h] = jnp.where(at == lane16 + h * 128, row16 + s * 16, found[h])
                for h in range(8):
                    inv[l, tokens, pl.ds(h * 128, 128)] = found[h]
            return carry

        lax.fori_loop(0, 8, step, 0)

    def prepare():
        gather_decoder(2, 4)
        for l in range(LAYERS):
            xt_ref[l] = jnp.transpose(xf[pl.ds(l, TOKENS, stride=4), :]).astype(BF16)
        loads[5].wait()
        loads[6].wait()
        goal_all = tgt_v[...].astype(F32)
        for c in range(2):
            goal[c] = goal_all[:, c, :]

    lax.fori_loop(0, LAYERS, gather, 0)
    pl.semaphore_wait(barrier, 23)
    exchange(ybuf, y, 4, ypeer, y_s, y_r, between=lambda: gather_decoder(0, 2))
    zbuf[zl] = total(ybuf, 4)
    exchange(zbuf, zl, 4, zpeer, z_s, z_r, between=prepare)
    val_v[...] = total(zbuf, 4).astype(BF16).astype(F32)

    def rebuild(b):
        zero = jnp.zeros((16, 128), F32)
        top, bottom = [], []
        for k in range(BLOCKS):
            row = val_v[pl.ds(source_of(k) * 8 + b, 1), :]
            block = jnp.where(mine, jnp.broadcast_to(row, (16, 128)), 0.0)
            if k == 0:
                top.append(block)
                bottom.append(zero)
            elif k == 1:
                top.append(block * jnp.where(g == 1, 1.0, 0.0))
                bottom.append(block * jnp.where(g == 1, 0.0, 1.0))
            else:
                top.append(zero)
                bottom.append(block)
        left = jnp.concatenate([jnp.concatenate(top, axis=1), jnp.concatenate(bottom, axis=1)],
                               axis=0)
        return jnp.dot(left.astype(BF16), rows_v[b],
                       preferred_element_type=F32).reshape(2, 16, FEAT)

    def give(i):
        other = lax.rem(q + i, 8)
        return send(rs_src.at[other], rs_buf.at[q], rs_s.at[i], rs_r.at[q], qpeer(i))

    order = (4, 3, 5, 2, 6, 1, 7)
    sends = []
    for n, i in enumerate(order):
        b = lax.rem(q + i, 8)
        rs_src[b] = rebuild(b).astype(BF16)
        if n > 0:
            sends.append(give(order[n - 1]))
    piece = rebuild(q)
    sends.append(give(order[-1]))
    build_inverse()
    for i in (1, 7, 2, 6, 3, 5, 4):
        other = lax.rem(q + i, 8)
        arrive(rs_buf, other, rs_s.at[i], rs_r.at[other], qpeer(i))
        piece = piece + rs_buf[other].astype(F32)
    hbuf[zh] = piece.astype(BF16)
    copy = send(hbuf.at[zh], hbuf.at[zh], h_s, h_r.at[zh], hpeer)
    def spread(b, carry):
        for l in range(LAYERS):
            scatter(act_v, val_v, inv, l, b)
        return carry

    lax.fori_loop(0, 8, spread, 0)
    pending.extend(sends)
    arrive(hbuf, 1 - zh, h_s, h_r.at[1 - zh], hpeer)
    pending.append(copy)
    rebuilt = total(hbuf, 2)
    for c in range(2):
        abuf[q, c] = (rebuilt[c] + dbias_v[pl.ds(c, 1), :] - goal[c]).astype(BF16)

    def back(b):
        out = lax.dot_general(abuf[b].reshape(32, FEAT), rows_v[b], (((1,), (1,)), ((), ())),
                              preferred_element_type=F32)

        def part(c, k):
            block = out[c * 16:c * 16 + 16, k * 128:k * 128 + 128]
            return jnp.sum(jnp.where(mine, block, 0.0), axis=0, keepdims=True)

        p0 = part(0, 0)
        p1 = jnp.where(g == 1, part(0, 1), part(1, 1))
        p2, p3, p4 = part(1, 2), part(1, 3), part(1, 4)
        pay_v[pl.ds(b, 1), :] = p0 + jnp.where(g == 1, p2, p1)
        pay_v[pl.ds(8 + b, 1), :] = jnp.where(g == 1, p1 + p3, p2)
        pay_v[pl.ds(16 + b, 1), :] = jnp.where(g == 1, p4, p3)
        pay_v[pl.ds(24 + b, 1), :] = jnp.where(g == 1, jnp.zeros_like(p4), p4)

    sends = [send(abuf.at[q], abuf.at[q], ag_s.at[i], ag_r.at[q], qpeer(i)) for i in order]
    back(q)
    for i in (1, 7, 2, 6, 3, 5, 4):
        other = lax.rem(q + i, 8)
        arrive(abuf, other, ag_s.at[i], ag_r.at[other], qpeer(i))
        back(other)
    pending.extend(sends)
    lbuf[r] = pay_v[...].astype(BF16)

    def decoder_grads():
        for k in range(BLOCKS):
            residue = abuf[:, jnp.where(k <= g, 0, 1)].reshape(TOKENS, FEAT)
            dg_ref[k] = lax.dot_general(act_v[source_of(k)], residue, (((0,), (0,)), ((), ())),
                                        preferred_element_type=F32)

    exchange(lbuf, r, 16, lpeer, l_s, l_r, between=decoder_grads)
    pick_ref[...] = total(lbuf, 16).astype(BF16).astype(F32)
    for copy in pending:
        copy.wait_send()


def main_call(x, enc, bias, dec, dbias, tgt, idx):
    dma = pltpu.SemaphoreType.DMA
    vmem = pltpu.VMEM
    return pl.pallas_call(
        main_kernel,
        out_shape=(
            jax.ShapeDtypeStruct((BLOCKS, WIDTH, FEAT), F32),
            jax.ShapeDtypeStruct((32, 128), F32),
            jax.ShapeDtypeStruct((LAYERS, TOKENS, WIDTH), I32),
            jax.ShapeDtypeStruct((LAYERS, DIN, TOKENS), BF16),
        ),
        in_specs=[pl.BlockSpec(memory_space=pltpu.HBM)] * 7,
        out_specs=(pl.BlockSpec(memory_space=pltpu.VMEM),) * 4,
        scratch_shapes=[
            vmem((TOKENS * LAYERS, DIN), BF16),
            vmem((LAYERS, DIN, WIDTH), BF16),
            vmem((LAYERS, WIDTH), F32),
            vmem((BLOCKS, WIDTH, FEAT), BF16),
            vmem((2, FEAT), F32),
            vmem((16, 2, FEAT), BF16),
            vmem((LAYERS, TOPK, TOKENS), I32),
            dma((7,)),
            vmem((TOKENS * LAYERS, DIN), F32),
            vmem((LAYERS, TOKENS, WIDTH), F32),
            vmem((LAYERS, TOKENS, 128), I32),
            vmem((LAYERS, TOKENS, 128), I32),
            vmem((LAYERS, TOKENS, 128), I32),
            vmem((LAYERS, 128, WIDTH), BF16),
            vmem((LAYERS, 128, WIDTH), BF16),
            vmem((8, BLOCKS * 128, FEAT), BF16),
            vmem((32, 128), F32),
            vmem((32, 128), F32),
            vmem((2, 16, FEAT), F32),
            vmem((LAYERS, TOKENS, WIDTH), BF16),
            vmem((4, 32, 128), F32),
            vmem((4, 32, 128), F32),
            vmem((16, 32, 128), BF16),
            vmem((8, 2, 16, FEAT), BF16),
            vmem((8, 2, 16, FEAT), BF16),
            vmem((2, 2, 16, FEAT), BF16),
            vmem((8, 2, 16, FEAT), BF16),
            dma((4,)), dma((4,)), dma((4,)), dma((4,)), dma((16,)), dma((16,)),
            dma((8,)), dma((8,)), dma, dma((2,)), dma((8,)), dma((8,)),
        ],
        compiler_params=pltpu.CompilerParams(collective_id=0, has_side_effects=True,
                                             vmem_limit_bytes=28 * 2**20),
        name="transcoder",
    )(*[pltpu.with_memory_space_constraint(v, pltpu.HBM)
        for v in (x, enc, bias, dec, dbias, tgt, idx)])


def grad_kernel(dg_ref, pick_ref, inv_ref, xt_ref, dg_hbm, eg_hbm, bg_ref, eg_v, pg_v, sem):
    copies = [pltpu.make_async_copy(dg_ref.at[k], dg_hbm.at[k], sem.at[k])
              for k in range(BLOCKS)]
    for copy in copies:
        copy.start()

    def layer(l, carry):
        for b in range(8):
            scatter(pg_v, pick_ref, inv_ref, l, b)
        grads = pg_v[l]
        eg_v[l] = jnp.dot(xt_ref[l], grads, preferred_element_type=F32)
        pltpu.make_async_copy(eg_v.at[l], eg_hbm.at[l], sem.at[BLOCKS + l]).start()
        bg_ref[pl.ds(l, 1), :] = jnp.dot(jnp.ones((8, TOKENS), BF16), grads,
                                         preferred_element_type=F32)[0:1]
        return carry

    lax.fori_loop(0, LAYERS, layer, 0)
    for l in range(LAYERS):
        pltpu.make_async_copy(eg_v.at[l], eg_hbm.at[l], sem.at[BLOCKS + l]).wait()
    for copy in copies:
        copy.wait()


def grad_call(dg, picked, inv, xt):
    vmem = pltpu.VMEM
    return pl.pallas_call(
        grad_kernel,
        out_shape=(
            jax.ShapeDtypeStruct((BLOCKS, WIDTH, FEAT), F32),
            jax.ShapeDtypeStruct((LAYERS, DIN, WIDTH), F32),
            jax.ShapeDtypeStruct((LAYERS, WIDTH), F32),
        ),
        in_specs=[pl.BlockSpec(memory_space=vmem)] * 4,
        out_specs=(pl.BlockSpec(memory_space=pl.ANY), pl.BlockSpec(memory_space=pl.ANY),
                   pl.BlockSpec(memory_space=vmem)),
        scratch_shapes=[vmem((LAYERS, DIN, WIDTH), F32),
                        vmem((LAYERS, TOKENS, WIDTH), BF16),
                        pltpu.SemaphoreType.DMA((BLOCKS + LAYERS,))],
        compiler_params=pltpu.CompilerParams(vmem_limit_bytes=24 * 2**20),
        name="weight_grads",
    )(dg, picked, inv, xt)


def body(inputs, encoder, enc_bias, decoder, dec_bias, targets, top_index):
    dg, picked, inv, xt = main_call(
        inputs.reshape(TOKENS * LAYERS, DIN), encoder, enc_bias, decoder[0], dec_bias[0],
        targets[0], jnp.transpose(top_index, (1, 2, 0)))
    dg, eg, bg = grad_call(dg, picked, inv, xt)
    return dg[None], eg, bg


def solution(mesh):
    return jax.shard_map(
        body,
        mesh=mesh,
        in_specs=(
            P(None, None, "layer"),
            P(None, "layer", "lat"),
            P(None, "lat"),
            P("layer", None, "lat", None),
            P("layer", None, None),
            P("layer", None, None, None),
            P(),
        ),
        out_specs=(P("layer", None, "lat", None), P(None, "layer", "lat"), P(None, "lat")),
        check_vma=False,
    )
```
